32 devices in a mesh: ctx: 4 (over y, x), tp: 4 (over z), dp: 2 (over core).
Axes of the slice: x: 2, y: 2, z: 4, core: 2. Of those that a mesh axis runs over, the one named last changes fastest.
Arguments:
- projected: bfloat16 [3, 2048, 4096], P(None, ('dp', 'ctx'), 'tp'), parts along dimension 1, may hold values from -6 to 6
- short_taps: float32 [3, 7, 4096], P(None, None, 'tp'), may hold values from -2 to 2
- long_filter: float32 [1024, 4096], P('ctx', 'tp'), may hold values from -2 to 2, as said below
- skip_gain: float32 [4096], P('tp'), may hold values from -1 to 1
- w_out: bfloat16 [4096, 4096], P('tp'), may hold values from -0.125 to 0.125
Outputs:
- hyena_out: bfloat16 [2048, 4096], P(('dp', 'ctx'), 'tp'), parts along dimension 0
The draws below stay inside these ranges and needn't reach their ends.
There are 2 independent parts, one for each index of `dp`. The reference program is written for one: setup_inputs(seed, part) draws one part's arguments, and reference() takes and returns one part's arrays. A program takes and returns all parts, laid end to end along the dimension named above; an argument that names none is the same for every part. Nothing has to cross between parts.
Inputs may be any that keep to these rules, and one draw needn't show every extreme that they name: `long_filter`: taps of each channel's causal filter.
All inputs are finite; a program needn't handle non-finite values.
Results may differ from the reference program's by a relative error of at most 0.014.
Values may be sent and summed in bfloat16 or wider, within the bound.
A program may use at most 64 MiB of HBM per device.

```python
import math
import jax
import jax.numpy as jnp
from jax import lax

D = 4096
TAPS = 7
SEQ = 1024


def draw_long_filter(key, part):
    key_noise = jax.random.fold_in(key, 11)
    key_rate = jax.random.fold_in(key, 12)
    key_kind = jax.random.fold_in(key, 13)
    fast_share = 0.5
    noise = jnp.clip(jax.random.normal(key_noise, (SEQ, D), jnp.float32), -5.0, 5.0)
    fast_mask = jax.random.bernoulli(key_kind, fast_share, (D,))
    unit_draw = jax.random.uniform(key_rate, (D,), jnp.float32)
    fast_rate = 1.0 / 50.0 * jnp.power(50.0 / 30.0, unit_draw)
    slow_rate = 0.1 / SEQ * jnp.power(20.0, unit_draw)
    rate_all = jnp.where(fast_mask, fast_rate, slow_rate)
    amplitude = jnp.sqrt(2.0 * rate_all + 1.0 / SEQ)
    positions = jnp.arange(SEQ, dtype=jnp.float32)[:, None]
    return (noise * amplitude[None, :] * jnp.exp(-rate_all[None, :] * positions)).astype(jnp.float32)


def strengthened(drawn, stream_key, source, target, shards_of, factor):
    def block_of(axis_at):
        return (jnp.arange(drawn.shape[axis_at]) // (drawn.shape[axis_at] // shards_of)).reshape((-1,) + (1,) * (drawn.ndim - 1 - axis_at))

    one_side = jax.random.permutation(stream_key, shards_of)[block_of(target)]
    far = (block_of(target) + shards_of // 2) % shards_of
    return jnp.where((block_of(source) == one_side) | (block_of(source) == far), factor * drawn, drawn)


def levels(own_key, shape, cuts, low, high):
    level = 1.0
    for axis_at, parts in cuts:
        steps = jax.random.uniform(jax.random.fold_in(jax.random.fold_in(own_key, 6), axis_at), (parts,), jnp.float32, low / len(cuts), high / len(cuts))
        level = level * jnp.repeat(jnp.exp(steps), shape[axis_at] // parts).reshape((-1,) + (1,) * (len(shape) - 1 - axis_at))
    return level


def centred(own_key, extent, scale, reach, pieces=(), kind=jnp.bfloat16):
    values = jax.random.normal(own_key, extent, jnp.float32) * scale
    if len(pieces) > 0:
        values = levels(own_key, extent, pieces, -0.22, 0.18) * values
    return jnp.clip(values, min=-reach, max=reach).astype(kind)


def gaussian_with(rng, dims, deviation, limit, cuts, heavy, kind=jnp.bfloat16):
    drawn = deviation * jax.random.normal(rng, dims, jnp.float32)
    if cuts:
        drawn = drawn * levels(rng, dims, cuts, -0.22, 0.18)
    return jnp.clip(strengthened(drawn, jax.random.fold_in(rng, 3), *heavy), -limit, limit).astype(kind)


def setup_inputs(seed: int = 0, part: int = 0) -> dict:
    arg_keys = jax.random.split(jax.random.key(seed), 6)
    part_splits = jax.random.split(jax.random.fold_in(arg_keys[5], part), 6)
    return {
        "projected": centred(part_splits[0], (3, SEQ, D), 1.0, 6.0, ((1, 4), (2, 4))),
        "short_taps": centred(arg_keys[1], (3, TAPS, D), TAPS ** -0.5, 2.0, ((2, 4),), jnp.float32),
        "long_filter": draw_long_filter(jax.random.fold_in(arg_keys[5], 71), part),
        "skip_gain": jnp.clip(jax.random.uniform(arg_keys[3], (D,), jnp.float32, -1.0, 1.0) * levels(arg_keys[3], (D,), ((0, 4),), -0.4, 0.0), -1.0, 1.0),
        "w_out": gaussian_with(arg_keys[4], (D, D), D ** -0.5, 0.125, ((0, 4),), (0, 1, 4, 2.0)),
    }


def featurize(inputs, taps):
    values = inputs.astype(jnp.float32)
    padded = jnp.pad(values, ((TAPS - 1, 0), (0, 0)))
    result = taps[0][None, :] * padded[TAPS - 1:TAPS - 1 + SEQ]
    for tap_index in range(1, TAPS):
        result = result + taps[tap_index][None, :] * padded[TAPS - 1 - tap_index:TAPS - 1 - tap_index + SEQ]
    return result


def reference(projected, short_taps, long_filter, skip_gain, w_out):
    query = featurize(projected[0], short_taps[0])
    keyed = featurize(projected[1], short_taps[1])
    valued = featurize(projected[2], short_taps[2])
    gated = keyed * valued
    block_width = math.gcd(D, 512)
    blocks = D // block_width
    span_len = 2 * SEQ

    def convolve(pair):
        gated_block, filter_block = pair
        spectrum = jnp.fft.rfft(gated_block, n=span_len, axis=0) * jnp.fft.rfft(filter_block, n=span_len, axis=0)
        return jnp.fft.irfft(spectrum, n=span_len, axis=0)[:SEQ].astype(gated_block.dtype)

    gated_blocks = gated.reshape(SEQ, blocks, block_width).transpose(1, 0, 2)
    filter_blocks = long_filter.reshape(SEQ, blocks, block_width).transpose(1, 0, 2)
    long_conv = lax.map(convolve, (gated_blocks, filter_blocks)).transpose(1, 0, 2).reshape(SEQ, D)
    mixed = (query * (long_conv + skip_gain[None, :] * gated)).astype(jnp.bfloat16)
    return jnp.dot(mixed, w_out, preferred_element_type=jnp.float32).astype(jnp.bfloat16)
```

```python
import functools
import math

import jax
import jax.numpy as jnp
import numpy as np
from jax import lax
from jax.experimental import pallas as pl
from jax.experimental.pallas import tpu as pltpu
from jax.sharding import PartitionSpec as P

TAPS = 7


exact_mode = lax.Precision.HIGHEST


def passed_along(block, axis, distance):
    devices = range(lax.axis_size(axis))
    route = [(i - distance, i) for i in devices if i - distance in devices]
    return lax.ppermute(block, axis, route)


def phase_table(left_index, right_index, period, sign_factor):
    turns = left_index * right_index % period
    angle = 2.0 * math.pi / period * turns.astype(jnp.float32)
    return (jnp.cos(angle), sign_factor * jnp.sin(angle))


def complex_apply(form, table_real, table_imag, data_real, data_imag):
    out_real = jnp.einsum(form, table_real, data_real, precision=exact_mode) - jnp.einsum(
        form, table_imag, data_imag, precision=exact_mode
    )
    out_imag = jnp.einsum(form, table_real, data_imag, precision=exact_mode) + jnp.einsum(
        form, table_imag, data_real, precision=exact_mode
    )
    return (out_real, out_imag)


def small_factor(length_all):
    factor = 1
    for candidate in range(1, length_all + 1):
        if candidate * candidate > length_all:
            break
        if length_all % candidate == 0:
            factor = candidate
    return factor


def local_dft(real_part, imag_part, sign_factor):
    dims_in = real_part.shape
    length_all = dims_in[-2]
    factor_one = small_factor(length_all)
    factor_two = length_all // factor_one
    leading = dims_in[:-2]
    channels = dims_in[-1]
    real_view = real_part.reshape(leading + (factor_one, factor_two, channels))
    imag_view = imag_part.reshape(leading + (factor_one, factor_two, channels))
    index_one = jnp.arange(factor_one, dtype=jnp.int32)
    index_two = jnp.arange(factor_two, dtype=jnp.int32)
    cos_one, sin_one = phase_table(index_one[:, None], index_one[None, :], factor_one, sign_factor)
    section_real, section_imag = complex_apply(
        "kn,...nmc->...kmc", cos_one, sin_one, real_view, imag_view
    )
    twist_real, twist_imag = phase_table(
        index_one[:, None], index_two[None, :], length_all, sign_factor
    )
    twist_real = twist_real[..., None]
    twist_imag = twist_imag[..., None]
    turned_real = section_real * twist_real - section_imag * twist_imag
    turned_imag = section_real * twist_imag + section_imag * twist_real
    cos_two, sin_two = phase_table(index_two[:, None], index_two[None, :], factor_two, sign_factor)
    final_real, final_imag = complex_apply(
        "dm,...kmc->...dkc", cos_two, sin_two, turned_real, turned_imag
    )
    return (final_real.reshape(dims_in), final_imag.reshape(dims_in))


def split_channels_conv(gated, long_filter):
    signals = jnp.stack([gated, long_filter])
    columns = lax.all_to_all(signals, "ctx", split_axis=2, concat_axis=1, tiled=True)
    whole_rows = columns.shape[1]
    total_len = 2 * whole_rows
    padded = jnp.concatenate([columns, jnp.zeros_like(columns)], axis=1)
    spec_real, spec_imag = local_dft(padded, jnp.zeros_like(padded), -1.0)
    prod_real = spec_real[0] * spec_real[1] - spec_imag[0] * spec_imag[1]
    prod_imag = spec_real[0] * spec_imag[1] + spec_imag[0] * spec_real[1]
    back_real, back_imag = local_dft(prod_real, prod_imag, 1.0)
    result_cols = back_real[:whole_rows] * (1.0 / total_len)
    return lax.all_to_all(result_cols, "ctx", split_axis=0, concat_axis=1, tiled=True)


def plain_local(projected, short_taps, long_filter, skip_gain, w_out):
    seq_rows = projected.shape[1]
    prior = passed_along(projected[:, seq_rows - (TAPS - 1) :, :], "ctx", 1)
    extended = jnp.concatenate([prior, projected], axis=1).astype(jnp.float32)
    featured = short_taps[:, 0, None, :] * extended[:, TAPS - 1 : TAPS - 1 + seq_rows, :]
    for tap_index in range(1, TAPS):
        featured = (
            featured
            + short_taps[:, tap_index, None, :]
            * extended[:, TAPS - 1 - tap_index : TAPS - 1 - tap_index + seq_rows, :]
        )
    query = featured[0]
    gated = featured[1] * featured[2]
    long_conv = split_channels_conv(gated, long_filter)
    mixed = (query * (long_conv + skip_gain[None, :] * gated)).astype(jnp.bfloat16)
    partial_terms = jnp.dot(mixed, w_out, preferred_element_type=jnp.float32)
    return lax.psum_scatter(
        partial_terms.astype(jnp.bfloat16), "tp", scatter_dimension=1, tiled=True
    )


HALO = 8
STRIP = 32
PIECES = 4
MESH_ID = pl.DeviceIdType.MESH


def block_tables(rows):
    length = 2 * rows
    k = np.arange(rows)[:, None]
    t = np.arange(rows)[None, :]
    angle = 2.0 * np.pi / length * (k * t % length)
    real, imag = np.cos(angle), -np.sin(angle)
    imag[0] = np.where(t[0] % 2 == 0, 1.0, -1.0)
    forward = np.concatenate([real, imag], axis=0)
    sign = np.where(k % 2 == 0, 1.0, -1.0)
    both = np.concatenate([forward * np.concatenate([sign, sign], axis=0), forward], axis=1)
    weight = np.where(k == 0, 1.0, 2.0) / length
    inverse = np.concatenate([real * weight, imag * weight], axis=0).T
    as_bf16 = lambda table: jnp.asarray(np.asarray(table, np.float32), jnp.bfloat16)
    return as_bf16(both), as_bf16(inverse)


def operator_kernel(
    n, m, p, proj, taps, filt, skip, w_hbm, both, inverse, out,
    halo, ext, gsend, hsend, hbuf, gall, gated, query, w, gspec, kspec, zspec,
    csend, conv, mixed, part, send_r, recv_r, send_l, recv_l,
    w_sem, halo_sem, h_ss, h_rs, f_ss, f_rs, g_ss, g_rs, c_ss, c_rs, r_ss, r_rs, l_ss, l_rs,
):
    me = lax.axis_index("ctx")
    z = lax.axis_index("tp")
    core = lax.axis_index("dp")
    rows, width = proj.shape[1], proj.shape[2]
    cols = width // n
    out_cols = out.shape[1]
    piece = rows // PIECES
    f32, bf16 = jnp.float32, jnp.bfloat16

    barrier = pltpu.get_barrier_semaphore()
    for k in range(1, n):
        pl.semaphore_signal(
            barrier, inc=1, device_id={"ctx": lax.rem(me + k, n)}, device_id_type=MESH_ID
        )

    for k in range(1, p):
        pl.semaphore_signal(
            barrier, inc=1, device_id={"dp": lax.rem(core + k, p)}, device_id_type=MESH_ID
        )

    @pl.when(z > 0)
    def _():
        pl.semaphore_signal(barrier, inc=1, device_id={"tp": z - 1}, device_id_type=MESH_ID)

    @pl.when(z < m - 1)
    def _():
        pl.semaphore_signal(barrier, inc=1, device_id={"tp": z + 1}, device_id_type=MESH_ID)

    w_copy = pltpu.make_async_copy(w_hbm, w, w_sem)
    w_copy.start()

    for c in range(n):
        hsend[c] = filt[:, c * cols : (c + 1) * cols].astype(bf16)
    hbuf[0] = jnp.zeros((rows, cols), bf16)
    hbuf[me + 1] = hsend[me]

    beside = jnp.where(z > 0, 1, 0) + jnp.where(z < m - 1, 1, 0)
    pl.semaphore_wait(barrier, n - 1 + p - 1 + beside)

    halo_copy = pltpu.make_async_remote_copy(
        proj.at[:, rows - HALO :, :], halo, halo_sem.at[0], halo_sem.at[1],
        device_id={"ctx": lax.rem(me + 1, n)}, device_id_type=MESH_ID,
    )

    @pl.when(me < n - 1)
    def _():
        halo_copy.start()

    @pl.when(me == 0)
    def _():
        halo[...] = jnp.zeros_like(halo)

    share = cols // p
    mine = pl.ds(pl.multiple_of(core * share, share), share)

    def h_copy(k):
        c = lax.rem(me + k, n)
        return pltpu.make_async_remote_copy(
            hsend.at[c, :, mine], hbuf.at[me + 1, :, mine], h_ss.at[k], h_rs.at[k],
            device_id={"ctx": c}, device_id_type=MESH_ID,
        )

    def f_copy(k, q):
        b = lax.rem(me + n - k, n) + 1
        return pltpu.make_async_remote_copy(
            hbuf.at[b, :, mine], hbuf.at[b, :, mine], f_ss.at[k, q], f_rs.at[k, q],
            device_id={"dp": lax.rem(core + q, p)}, device_id_type=MESH_ID,
        )

    def g_copy(k):
        c = lax.rem(me + k, n)
        return pltpu.make_async_remote_copy(
            gsend.at[c], gall.at[me], g_ss.at[k], g_rs.at[k],
            device_id={"ctx": c}, device_id_type=MESH_ID,
        )

    def c_copy(r, k):
        c = lax.rem(me + k, n)
        span = pl.ds(pl.multiple_of(r * piece, piece), piece)
        return pltpu.make_async_remote_copy(
            csend.at[c, span], conv.at[me, span], c_ss.at[r, k], c_rs.at[r, k],
            device_id={"ctx": c}, device_id_type=MESH_ID,
        )

    def r_copy(d, r):
        span = pl.ds(pl.multiple_of(r * piece, piece), piece)
        return pltpu.make_async_remote_copy(
            send_r.at[d, span], recv_r.at[d, span], r_ss.at[d, r], r_rs.at[d, r],
            device_id={"tp": lax.rem(z + 1, m)}, device_id_type=MESH_ID,
        )

    def l_copy(d, r):
        span = pl.ds(pl.multiple_of(r * piece, piece), piece)
        return pltpu.make_async_remote_copy(
            send_l.at[d, span], recv_l.at[d, span], l_ss.at[d, r], l_rs.at[d, r],
            device_id={"tp": lax.rem(z + m - 1, m)}, device_id_type=MESH_ID,
        )

    for k in range(1, n):
        h_copy(k).start()

    def features(i, start, span):
        total = None
        for j in range(TAPS):
            term = taps[i, pl.ds(j, 1), span] * ext[i, pl.ds(HALO + start - j, STRIP), :]
            total = term if total is None else total + term
        return total

    def fill_body(i, span):
        ext[i, HALO:, :] = proj[i, :, span].astype(f32)

    def fill_head(i, span):
        ext[i, :HALO, :] = halo[i, :, span].astype(f32)

    def gate_block(k, _):
        c = lax.rem(me + 1 + k, n)
        span = pl.ds(pl.multiple_of(c * cols, cols), cols)
        fill_body(1, span)
        fill_body(2, span)

        def strip(start):
            value = features(1, start, span) * features(2, start, span)
            gated[start : start + STRIP, span] = value
            gsend[c, start : start + STRIP, :] = value.astype(bf16)

        for start in reversed(range(STRIP, rows, STRIP)):
            strip(start)

        @pl.when((k == 0) & (me > 0))
        def _():
            halo_copy.wait_recv()

        fill_head(1, span)
        fill_head(2, span)
        strip(0)

        @pl.when(k < n - 1)
        def _():
            g_copy(k + 1).start()

        return 0

    lax.fori_loop(0, n, gate_block, 0)
    gall[me] = gsend[me]

    def query_block(c, _):
        span = pl.ds(pl.multiple_of(c * cols, cols), cols)
        fill_body(0, span)
        fill_head(0, span)
        for start in range(0, rows, STRIP):
            query[start : start + STRIP, span] = features(0, start, span)
        return 0

    for k in range(1, n):
        h_copy(k).wait_recv()
        for q in range(1, p):
            f_copy(k, q).start()

    lax.fori_loop(0, n, query_block, 0)

    for k in range(1, n):
        for q in range(1, p):
            f_copy(k, q).wait_recv()

    first_row = lax.broadcasted_iota(jnp.int32, (rows, cols), 0) == 0

    def filter_spectrum(b, _):
        pair = hbuf[pl.ds(b, 2)].reshape(2 * rows, cols)
        spec = jnp.dot(both[...], pair, preferred_element_type=f32)
        real, imag = spec[:rows], spec[rows:]
        kspec[b, 0] = real
        kspec[b, 1] = jnp.where(first_row, 0.0, imag)
        kspec[b, 2] = jnp.where(first_row, imag, real)
        return 0

    lax.fori_loop(0, n, filter_spectrum, 0)

    for k in range(1, n):
        g_copy(k).wait_recv()

    def signal_spectrum(b, _):
        gspec[b] = jnp.dot(both[:, rows:], gall[b], preferred_element_type=f32)
        return 0

    lax.fori_loop(0, n, signal_spectrum, 0)

    def product(s, _):
        real_at = pl.ds(pl.multiple_of(s * 16, 16), 16)
        imag_at = pl.ds(pl.multiple_of(rows + s * 16, 16), 16)
        for lane in range(0, cols, 128):
            lanes = slice(lane, lane + 128)
            g_re = [gspec[b, real_at, lanes] for b in range(n)]
            g_im = [gspec[b, imag_at, lanes] for b in range(n)]
            k_re = [kspec[b, 0, real_at, lanes] for b in range(n)]
            k_im = [kspec[b, 1, real_at, lanes] for b in range(n)]
            k_alt = [kspec[b, 2, real_at, lanes] for b in range(n)]
            for i in range(n):
                z_re = z_im = None
                for j in range(i + 1):
                    t_re = g_re[j] * k_re[i - j] - g_im[j] * k_im[i - j]
                    t_im = g_re[j] * k_im[i - j] + g_im[j] * k_alt[i - j]
                    z_re = t_re if z_re is None else z_re + t_re
                    z_im = t_im if z_im is None else z_im + t_im
                zspec[i, real_at, lanes] = z_re.astype(bf16)
                zspec[i, imag_at, lanes] = z_im.astype(bf16)
        return 0

    lax.fori_loop(0, rows // 16, product, 0)

    def back(index, _):
        r = index // n
        k = index % n
        c = lax.rem(me + 1 + k, n)
        span = pl.ds(pl.multiple_of(r * piece, piece), piece)
        value = jnp.dot(inverse[span, :], zspec[c], preferred_element_type=f32)
        csend[c, span, :] = value.astype(bf16)

        @pl.when(k < n - 1)
        def _():
            c_copy(r, k + 1).start()

        @pl.when(k == n - 1)
        def _():
            conv[me, span, :] = value.astype(bf16)

        return 0

    lax.fori_loop(0, PIECES * n, back, 0)
    w_copy.wait()

    tile = math.gcd(out_cols, 256)
    def tail(r, _):
        @pl.when(r < PIECES)
        def _():
            span = pl.ds(pl.multiple_of(r * piece, piece), piece)
            for k in range(1, n):
                c_copy(r, k).wait_recv()
            for c in range(n):
                at = slice(c * cols, (c + 1) * cols)
                mixed[span, at] = (
                    query[span, at]
                    * (conv[c, span, :].astype(f32) + skip[:, at] * gated[span, at])
                ).astype(bf16)
            for s in range(m):
                d = jnp.where(2 * z < m, m - 1 - s, s)

                def one(t, _):
                    w_at = pl.ds(pl.multiple_of(d * out_cols + t * tile, tile), tile)
                    p_at = pl.ds(pl.multiple_of(t * tile, tile), tile)
                    value = jnp.dot(mixed[span, :], w[:, w_at], preferred_element_type=jnp.float32)
                    part[d, span, p_at] = value
                    return 0

                lax.fori_loop(0, out_cols // tile, one, 0)

                @pl.when((z == 0) & (d > 0))
                def _():
                    send_r[d, span, :] = part[d, span, :].astype(bf16)
                    r_copy(d, r).start()

                @pl.when((z == m - 1) & (d < m - 1))
                def _():
                    send_l[d, span, :] = part[d, span, :].astype(bf16)
                    l_copy(d, r).start()

        @pl.when((r >= 1) & (r < PIECES + 1))
        def _():
            q = r - 1
            span = pl.ds(pl.multiple_of(q * piece, piece), piece)

            def relay_right():
                for d in reversed(range(1, m)):
                    @pl.when((z > 0) & (z < d))
                    def _():
                        r_copy(d, q).wait_recv()
                        send_r[d, span, :] = (
                            part[d, span, :] + recv_r[d, span, :].astype(f32)
                        ).astype(bf16)
                        r_copy(d, q).start()

            def relay_left():
                for d in range(m - 1):
                    @pl.when((z < m - 1) & (z > d))
                    def _():
                        l_copy(d, q).wait_recv()
                        send_l[d, span, :] = (
                            part[d, span, :] + recv_l[d, span, :].astype(f32)
                        ).astype(bf16)
                        l_copy(d, q).start()

            pl.when(2 * z < m)(relay_right)
            relay_left()
            pl.when(2 * z >= m)(relay_right)

        @pl.when(r >= 2)
        def _():
            q = r - 2
            span = pl.ds(pl.multiple_of(q * piece, piece), piece)

            @pl.when(z > 0)
            def _():
                r_copy(z, q).wait_recv()
                part[z, span, :] = part[z, span, :] + recv_r[z, span, :].astype(f32)

            @pl.when(z < m - 1)
            def _():
                l_copy(z, q).wait_recv()
                part[z, span, :] = part[z, span, :] + recv_l[z, span, :].astype(f32)

            out[span, :] = part[z, span, :].astype(bf16)

        return 0

    lax.fori_loop(0, PIECES + 2, tail, 0)

    @pl.when(me < n - 1)
    def _():
        halo_copy.wait_send()

    for k in range(1, n):
        h_copy(k).wait_send()
        for q in range(1, p):
            f_copy(k, q).wait_send()
        g_copy(k).wait_send()
        for r in range(PIECES):
            c_copy(r, k).wait_send()
    for d in range(m):
        for r in range(PIECES):
            @pl.when(z < d)
            def _():
                r_copy(d, r).wait_send()

            @pl.when(z > d)
            def _():
                l_copy(d, r).wait_send()


def fused_local(n, m, p, projected, short_taps, long_filter, skip_gain, w_out):
    rows, width = projected.shape[1:]
    cols = width // n
    out_cols = w_out.shape[1] // m
    both, inverse = block_tables(rows)
    f32, bf16 = jnp.float32, jnp.bfloat16
    vmem = pl.BlockSpec(memory_space=pltpu.VMEM)
    dma = pltpu.SemaphoreType.DMA
    blocks = lambda kind: pltpu.VMEM((n, rows, cols), kind)
    sums = lambda kind: pltpu.VMEM((m, rows, out_cols), kind)
    return pl.pallas_call(
        functools.partial(operator_kernel, n, m, p),
        out_shape=jax.ShapeDtypeStruct((rows, out_cols), bf16),
        in_specs=[vmem, vmem, vmem, vmem, pl.BlockSpec(memory_space=pl.ANY), vmem, vmem],
        out_specs=vmem,
        scratch_shapes=[
            pltpu.VMEM((3, HALO, width), bf16),
            pltpu.VMEM((3, HALO + rows, cols), f32),
            blocks(bf16),
            blocks(bf16),
            pltpu.VMEM((n + 1, rows, cols), bf16),
            blocks(bf16),
            pltpu.VMEM((rows, width), f32),
            pltpu.VMEM((rows, width), f32),
            pltpu.VMEM(w_out.shape, bf16),
            pltpu.VMEM((n, 2 * rows, cols), f32),
            pltpu.VMEM((n, 3, rows, cols), f32),
            pltpu.VMEM((n, 2 * rows, cols), bf16),
            blocks(bf16),
            blocks(bf16),
            pltpu.VMEM((rows, width), bf16),
            sums(f32),
            sums(bf16),
            sums(bf16),
            sums(bf16),
            sums(bf16),
            dma,
            dma((2,)),
            dma((n,)),
            dma((n,)),
            dma((n, p)),
            dma((n, p)),
            dma((n,)),
            dma((n,)),
            dma((PIECES, n)),
            dma((PIECES, n)),
            dma((m, PIECES)),
            dma((m, PIECES)),
            dma((m, PIECES)),
            dma((m, PIECES)),
        ],
        compiler_params=pltpu.CompilerParams(
            collective_id=0, has_side_effects=True, vmem_limit_bytes=60 * 1024 * 1024
        ),
    )(projected, short_taps, long_filter, skip_gain.reshape(1, width), w_out, both, inverse)


def fits_kernel(n, m, p, rows, width, all_out):
    if n < 2 or m < 2 or width % (128 * n * p) or all_out % (128 * m):
        return False
    if rows % (16 * PIECES) or rows % STRIP:
        return False
    held = 35 * rows * width + 12 * rows * all_out + 2 * width * all_out + 12 * rows * rows
    return held + 4 * rows * width + 4 * 1024 * 1024 < 60 * 1024 * 1024


def local(n, m, p, projected, short_taps, long_filter, skip_gain, w_out):
    rows, width = projected.shape[1:]
    if fits_kernel(n, m, p, rows, width, w_out.shape[1]):
        return fused_local(n, m, p, projected, short_taps, long_filter, skip_gain, w_out)
    return plain_local(projected, short_taps, long_filter, skip_gain, w_out)


def solution(mesh):
    in_specs = (
        P(None, ("dp", "ctx"), "tp"),
        P(None, None, "tp"),
        P("ctx", "tp"),
        P("tp"),
        P("tp", None),
    )
    out_specs = P(("dp", "ctx"), "tp")
    body = functools.partial(local, mesh.shape["ctx"], mesh.shape["tp"], mesh.shape["dp"])
    return jax.shard_map(body, mesh=mesh, in_specs=in_specs, out_specs=out_specs, check_vma=False)
```

```python
import functools
import math

import jax
import jax.numpy as jnp
import numpy as np
from jax import lax
from jax.experimental import pallas as pl
from jax.experimental.pallas import tpu as pltpu
from jax.sharding import PartitionSpec as P

TAPS = 7


exact_mode = lax.Precision.HIGHEST


def passed_along(block, axis, distance):
    devices = range(lax.axis_size(axis))
    route = [(i - distance, i) for i in devices if i - distance in devices]
    return lax.ppermute(block, axis, route)


def phase_table(left_index, right_index, period, sign_factor):
    turns = left_index * right_index % period
    angle = 2.0 * math.pi / period * turns.astype(jnp.float32)
    return (jnp.cos(angle), sign_factor * jnp.sin(angle))


def complex_apply(form, table_real, table_imag, data_real, data_imag):
    out_real = jnp.einsum(form, table_real, data_real, precision=exact_mode) - jnp.einsum(
        form, table_imag, data_imag, precision=exact_mode
    )
    out_imag = jnp.einsum(form, table_real, data_imag, precision=exact_mode) + jnp.einsum(
        form, table_imag, data_real, precision=exact_mode
    )
    return (out_real, out_imag)


def small_factor(length_all):
    factor = 1
    for candidate in range(1, length_all + 1):
        if candidate * candidate > length_all:
            break
        if length_all % candidate == 0:
            factor = candidate
    return factor


def local_dft(real_part, imag_part, sign_factor):
    dims_in = real_part.shape
    length_all = dims_in[-2]
    factor_one = small_factor(length_all)
    factor_two = length_all // factor_one
    leading = dims_in[:-2]
    channels = dims_in[-1]
    real_view = real_part.reshape(leading + (factor_one, factor_two, channels))
    imag_view = imag_part.reshape(leading + (factor_one, factor_two, channels))
    index_one = jnp.arange(factor_one, dtype=jnp.int32)
    index_two = jnp.arange(factor_two, dtype=jnp.int32)
    cos_one, sin_one = phase_table(index_one[:, None], index_one[None, :], factor_one, sign_factor)
    section_real, section_imag = complex_apply(
        "kn,...nmc->...kmc", cos_one, sin_one, real_view, imag_view
    )
    twist_real, twist_imag = phase_table(
        index_one[:, None], index_two[None, :], length_all, sign_factor
    )
    twist_real = twist_real[..., None]
    twist_imag = twist_imag[..., None]
    turned_real = section_real * twist_real - section_imag * twist_imag
    turned_imag = section_real * twist_imag + section_imag * twist_real
    cos_two, sin_two = phase_table(index_two[:, None], index_two[None, :], factor_two, sign_factor)
    final_real, final_imag = complex_apply(
        "dm,...kmc->...dkc", cos_two, sin_two, turned_real, turned_imag
    )
    return (final_real.reshape(dims_in), final_imag.reshape(dims_in))


def split_channels_conv(gated, long_filter):
    signals = jnp.stack([gated, long_filter])
    columns = lax.all_to_all(signals, "ctx", split_axis=2, concat_axis=1, tiled=True)
    whole_rows = columns.shape[1]
    total_len = 2 * whole_rows
    padded = jnp.concatenate([columns, jnp.zeros_like(columns)], axis=1)
    spec_real, spec_imag = local_dft(padded, jnp.zeros_like(padded), -1.0)
    prod_real = spec_real[0] * spec_real[1] - spec_imag[0] * spec_imag[1]
    prod_imag = spec_real[0] * spec_imag[1] + spec_imag[0] * spec_real[1]
    back_real, back_imag = local_dft(prod_real, prod_imag, 1.0)
    result_cols = back_real[:whole_rows] * (1.0 / total_len)
    return lax.all_to_all(result_cols, "ctx", split_axis=0, concat_axis=1, tiled=True)


def plain_local(projected, short_taps, long_filter, skip_gain, w_out):
    seq_rows = projected.shape[1]
    prior = passed_along(projected[:, seq_rows - (TAPS - 1) :, :], "ctx", 1)
    extended = jnp.concatenate([prior, projected], axis=1).astype(jnp.float32)
    featured = short_taps[:, 0, None, :] * extended[:, TAPS - 1 : TAPS - 1 + seq_rows, :]
    for tap_index in range(1, TAPS):
        featured = (
            featured
            + short_taps[:, tap_index, None, :]
            * extended[:, TAPS - 1 - tap_index : TAPS - 1 - tap_index + seq_rows, :]
        )
    query = featured[0]
    gated = featured[1] * featured[2]
    long_conv = split_channels_conv(gated, long_filter)
    mixed = (query * (long_conv + skip_gain[None, :] * gated)).astype(jnp.bfloat16)
    partial_terms = jnp.dot(mixed, w_out, preferred_element_type=jnp.float32)
    return lax.psum_scatter(
        partial_terms.astype(jnp.bfloat16), "tp", scatter_dimension=1, tiled=True
    )


HALO = 8
STRIP = 32
PIECES = 4
UNITS = 8
HANDED = 2
LIMIT = 60 * 1024 * 1024
MESH_ID = pl.DeviceIdType.MESH


def block_tables(rows):
    length = 2 * rows
    k = np.arange(rows)[:, None]
    t = np.arange(rows)[None, :]
    angle = 2.0 * np.pi / length * (k * t % length)
    real, imag = np.cos(angle), -np.sin(angle)
    imag[0] = np.where(t[0] % 2 == 0, 1.0, -1.0)
    forward = np.concatenate([real, imag], axis=0)
    sign = np.where(k % 2 == 0, 1.0, -1.0)
    both = np.concatenate([forward * np.concatenate([sign, sign], axis=0), forward], axis=1)
    weight = np.where(k == 0, 1.0, 2.0) / length
    inverse = np.concatenate([real * weight, imag * weight], axis=0).T
    as_bf16 = lambda table: jnp.asarray(np.asarray(table, np.float32), jnp.bfloat16)
    return as_bf16(both), as_bf16(inverse)


def operator_kernel(
    n, m, p, proj_hbm, taps_hbm, filt_hbm, skip_hbm, w_hbm, both_hbm, inverse_hbm, out_hbm,
    proj, taps, filt, skip, both, inverse, w, out,
    halo, ext, gsend, hsend, hbuf, gall, gated, query, gspec, kspec, zspec,
    csend, conv, mixed, part, near_s, near_r, mix_r, far_s, far_r, home_s, home_r, handed,
    load_sem, out_sem, halo_sem, h_ss, h_rs, f_ss, f_rs, g_ss, g_rs, c_ss, c_rs,
    near_ss, near_rs, mix_ss, mix_rs, far_ss, far_rs, home_ss, home_rs,
    w_ss, w_rs, s_ss, s_rs, b_ss, b_rs,
):
    me = lax.axis_index("ctx")
    z = lax.axis_index("tp")
    core = lax.axis_index("dp")
    rows, width = proj.shape[1], proj.shape[2]
    cols = width // n
    out_cols = out.shape[1]
    piece = rows // PIECES
    unit = rows // UNITS
    f32, bf16 = jnp.float32, jnp.bfloat16

    lower = 2 * z < m
    inner = jnp.where(lower, z, m - 1 - z)
    at_end = inner == 0
    at_mid = inner == 1
    pair = z + 1 - 2 * lax.rem(z, 2)
    across = m - 1 - z

    barrier = pltpu.get_barrier_semaphore()
    for k in range(1, n):
        pl.semaphore_signal(
            barrier, inc=1, device_id={"ctx": lax.rem(me + k, n)}, device_id_type=MESH_ID
        )
    for k in range(1, p):
        pl.semaphore_signal(
            barrier, inc=1, device_id={"dp": lax.rem(core + k, p)}, device_id_type=MESH_ID
        )
    pl.semaphore_signal(barrier, inc=1, device_id={"tp": pair}, device_id_type=MESH_ID)

    @pl.when(at_mid)
    def _():
        pl.semaphore_signal(barrier, inc=1, device_id={"tp": across}, device_id_type=MESH_ID)

    pairs = (
        (filt_hbm, filt), (proj_hbm, proj), (taps_hbm, taps), (both_hbm, both),
        (inverse_hbm, inverse), (skip_hbm, skip), (w_hbm, w),
    )
    loads = [pltpu.make_async_copy(a, b, load_sem.at[i]) for i, (a, b) in enumerate(pairs)]
    filt_load, proj_load, taps_load, both_load, inverse_load, skip_load, w_load = loads
    for load in loads:
        load.start()

    filt_load.wait()
    for c in range(n):
        hsend[c] = filt[:, c * cols : (c + 1) * cols].astype(bf16)
    hbuf[0] = jnp.zeros((rows, cols), bf16)
    hbuf[me + 1] = hsend[me]
    proj_load.wait()

    pl.semaphore_wait(barrier, n - 1 + p - 1 + 1 + jnp.where(at_mid, 1, 0))

    halo_copy = pltpu.make_async_remote_copy(
        proj.at[:, rows - HALO :, :], halo, halo_sem.at[0], halo_sem.at[1],
        device_id={"ctx": lax.rem(me + 1, n)}, device_id_type=MESH_ID,
    )

    @pl.when(me < n - 1)
    def _():
        halo_copy.start()

    @pl.when(me == 0)
    def _():
        halo[...] = jnp.zeros_like(halo)

    share = cols // p
    mine = pl.ds(pl.multiple_of(core * share, share), share)
    group = width // (n * p)

    def whole(index, size):
        return pl.ds(pl.multiple_of(index * size, size), size)

    def real(d):
        return jnp.where(lower, d, m - 1 - d)

    def block(d):
        return whole(real(d), out_cols)

    def h_copy(k):
        c = lax.rem(me + k, n)
        return pltpu.make_async_remote_copy(
            hsend.at[c, :, mine], hbuf.at[me + 1, :, mine], h_ss.at[k], h_rs.at[k],
            device_id={"ctx": c}, device_id_type=MESH_ID,
        )

    def f_copy(k, q):
        b = lax.rem(me + n - k, n) + 1
        return pltpu.make_async_remote_copy(
            hbuf.at[b, :, mine], hbuf.at[b, :, mine], f_ss.at[k, q], f_rs.at[k, q],
            device_id={"dp": lax.rem(core + q, p)}, device_id_type=MESH_ID,
        )

    def g_copy(k):
        c = lax.rem(me + k, n)
        return pltpu.make_async_remote_copy(
            gsend.at[c], gall.at[me], g_ss.at[k], g_rs.at[k],
            device_id={"ctx": c}, device_id_type=MESH_ID,
        )

    def c_copy(r, k):
        c = lax.rem(me + k, n)
        span = whole(r, piece)
        return pltpu.make_async_remote_copy(
            csend.at[c, span], conv.at[me, span], c_ss.at[r, k], c_rs.at[r, k],
            device_id={"ctx": c}, device_id_type=MESH_ID,
        )

    def near_copy(u):
        return pltpu.make_async_remote_copy(
            near_s.at[whole(u, unit)], near_r.at[whole(u, unit)], near_ss.at[u], near_rs.at[u],
            device_id={"tp": pair}, device_id_type=MESH_ID,
        )

    def mix_copy(u):
        return pltpu.make_async_remote_copy(
            mixed.at[whole(u, unit)], mix_r.at[whole(u, unit)], mix_ss.at[u], mix_rs.at[u],
            device_id={"tp": pair}, device_id_type=MESH_ID,
        )

    def far_copy(v):
        return pltpu.make_async_remote_copy(
            far_s.at[whole(v, unit)], far_r.at[whole(v, unit)], far_ss.at[v], far_rs.at[v],
            device_id={"tp": across}, device_id_type=MESH_ID,
        )

    def home_copy(u):
        return pltpu.make_async_remote_copy(
            home_s.at[whole(u, unit)], home_r.at[whole(u, unit)], home_ss.at[u], home_rs.at[u],
            device_id={"tp": pair}, device_id_type=MESH_ID,
        )

    def own_group(k):
        return whole(lax.rem(me + n - k, n) * p + core, group)

    def w_copy(j):
        return pltpu.make_async_remote_copy(
            w_hbm.at[own_group(0), block(m - 2 - j)], handed.at[j, own_group(0)],
            w_ss.at[j], w_rs.at[j], device_id={"tp": pair}, device_id_type=MESH_ID,
        )

    def s_copy(j, k):
        return pltpu.make_async_remote_copy(
            handed.at[j, own_group(0)], handed.at[j, own_group(0)], s_ss.at[j, k], s_rs.at[j, k],
            device_id={"ctx": lax.rem(me + k, n)}, device_id_type=MESH_ID,
        )

    def b_copy(j, k, q):
        return pltpu.make_async_remote_copy(
            handed.at[j, own_group(k)], handed.at[j, own_group(k)],
            b_ss.at[j, k, q], b_rs.at[j, k, q],
            device_id={"dp": lax.rem(core + q, p)}, device_id_type=MESH_ID,
        )

    def out_copy(u):
        return pltpu.make_async_copy(
            out.at[whole(u, unit)], out_hbm.at[whole(u, unit)], out_sem.at[u]
        )

    for k in range(1, n):
        h_copy(k).start()

    @pl.when(at_end)
    def _():
        for j in range(HANDED):
            w_copy(j).start()

    def features(i, start, span):
        total = None
        for j in range(TAPS):
            term = taps[i, pl.ds(j, 1), span] * ext[i, pl.ds(HALO + start - j, STRIP), :]
            total = term if total is None else total + term
        return total

    def fill_body(i, span):
        ext[i, HALO:, :] = proj[i, :, span].astype(f32)

    def fill_head(i, span):
        ext[i, :HALO, :] = halo[i, :, span].astype(f32)

    taps_load.wait()

    def gate_block(k, _):
        c = lax.rem(me + 1 + k, n)
        span = whole(c, cols)
        fill_body(1, span)
        fill_body(2, span)

        def strip(start):
            value = features(1, start, span) * features(2, start, span)
            gated[start : start + STRIP, span] = value
            gsend[c, start : start + STRIP, :] = value.astype(bf16)

        for start in reversed(range(STRIP, rows, STRIP)):
            strip(start)

        @pl.when((k == 0) & (me > 0))
        def _():
            halo_copy.wait_recv()

        fill_head(1, span)
        fill_head(2, span)
        strip(0)

        @pl.when(k < n - 1)
        def _():
            g_copy(k + 1).start()

        return 0

    lax.fori_loop(0, n, gate_block, 0)
    gall[me] = gsend[me]

    def query_block(c, _):
        span = whole(c, cols)
        fill_body(0, span)
        fill_head(0, span)
        for start in range(0, rows, STRIP):
            query[start : start + STRIP, span] = features(0, start, span)
        return 0

    for k in range(1, n):
        h_copy(k).wait_recv()
        for q in range(1, p):
            f_copy(k, q).start()

    lax.fori_loop(0, n, query_block, 0)

    for k in range(1, n):
        for q in range(1, p):
            f_copy(k, q).wait_recv()
    both_load.wait()

    first_row = lax.broadcasted_iota(jnp.int32, (rows, cols), 0) == 0

    def filter_spectrum(b, _):
        two = hbuf[pl.ds(b, 2)].reshape(2 * rows, cols)
        spec = jnp.dot(both[...], two, preferred_element_type=f32)
        re, im = spec[:rows], spec[rows:]
        kspec[b, 0] = re
        kspec[b, 1] = jnp.where(first_row, 0.0, im)
        kspec[b, 2] = jnp.where(first_row, im, re)
        return 0

    lax.fori_loop(0, n, filter_spectrum, 0)

    def signal_spectrum(k, _):
        b = lax.rem(me + n - k, n)

        @pl.when(k > 0)
        def _():
            g_copy(k).wait_recv()

        gspec[b] = jnp.dot(both[:, rows:], gall[b], preferred_element_type=f32)
        return 0

    lax.fori_loop(0, n, signal_spectrum, 0)

    def product(s, _):
        real_at = whole(s, 16)
        imag_at = pl.ds(pl.multiple_of(rows + s * 16, 16), 16)
        for lane in range(0, cols, 128):
            lanes = slice(lane, lane + 128)
            g_re = [gspec[b, real_at, lanes] for b in range(n)]
            g_im = [gspec[b, imag_at, lanes] for b in range(n)]
            k_re = [kspec[b, 0, real_at, lanes] for b in range(n)]
            k_im = [kspec[b, 1, real_at, lanes] for b in range(n)]
            k_alt = [kspec[b, 2, real_at, lanes] for b in range(n)]
            for i in range(n):
                z_re = z_im = None
                for j in range(i + 1):
                    t_re = g_re[j] * k_re[i - j] - g_im[j] * k_im[i - j]
                    t_im = g_re[j] * k_im[i - j] + g_im[j] * k_alt[i - j]
                    z_re = t_re if z_re is None else z_re + t_re
                    z_im = t_im if z_im is None else z_im + t_im
                zspec[i, real_at, lanes] = z_re.astype(bf16)
                zspec[i, imag_at, lanes] = z_im.astype(bf16)
        return 0

    lax.fori_loop(0, rows // 16, product, 0)
    inverse_load.wait()

    def back(index, _):
        r = index // n
        k = index % n
        c = lax.rem(me + 1 + k, n)
        span = whole(r, piece)
        value = jnp.dot(inverse[span, :], zspec[c], preferred_element_type=f32)
        csend[c, span, :] = value.astype(bf16)

        @pl.when(k < n - 1)
        def _():
            c_copy(r, k + 1).start()

        @pl.when(k == n - 1)
        def _():
            conv[me, span, :] = value.astype(bf16)

        return 0

    lax.fori_loop(0, PIECES * n, back, 0)
    skip_load.wait()
    w_load.wait()

    @pl.when(at_mid)
    def _():
        for j in range(HANDED):
            w_copy(j).wait_recv()
            for k in range(1, n):
                s_copy(j, k).start()
            for q in range(1, p):
                b_copy(j, 0, q).start()

    def mix_piece(r):
        span = whole(r, piece)
        for k in range(1, n):
            c_copy(r, k).wait_recv()
        for c in range(n):
            at = slice(c * cols, (c + 1) * cols)
            mixed[span, at] = (
                query[span, at]
                * (conv[c, span, :].astype(f32) + skip[:, at] * gated[span, at])
            ).astype(bf16)
        value = jnp.dot(mixed[span, :], w[:, block(m - 1)], preferred_element_type=f32)

        @pl.when(at_end)
        def _():
            near_s[span, :] = value.astype(bf16)
            for u in range(UNITS // PIECES):
                near_copy(r * (UNITS // PIECES) + u).start()

        @pl.when(at_mid)
        def _():
            part[m - 1, span, :] = value

    def own_part(d):
        part[d] = jnp.dot(mixed[...], w[:, block(d)], preferred_element_type=f32)

    def finish(u, value):
        out[whole(u, unit), :] = value.astype(bf16)
        out_copy(u).start()

    def ends():
        def first(r, _):
            mix_piece(r)
            return 0

        lax.fori_loop(0, PIECES, first, 0)

        def give(u, _):
            mix_copy(u).start()
            return 0

        lax.fori_loop(0, UNITS, give, 0)
        own_part(0)

        def last(u, _):
            home_copy(u).wait_recv()
            at = whole(u, unit)
            finish(u, part[0, at, :] + home_r[at, :].astype(f32))
            return 0

        lax.fori_loop(0, UNITS, last, 0)

    def take_handed(j):
        for k in range(1, n):
            s_copy(j, k).wait_recv()
            for q in range(1, p):
                b_copy(j, k, q).start()
        for k in range(n):
            for q in range(1, p):
                b_copy(j, k, q).wait_recv()

    def mids():
        def step(s, _):
            @pl.when(s < PIECES)
            def _():
                mix_piece(s)

            @pl.when(s == PIECES)
            def _():
                own_part(0)

            @pl.when(s == PIECES + 1)
            def _():
                own_part(2)

            @pl.when(s == PIECES + 2)
            def _():
                own_part(1)

            @pl.when(s == UNITS + 2)
            def _():
                take_handed(0)

            v = s - 2

            @pl.when((v >= 0) & (v < UNITS))
            def _():
                at = whole(v, unit)
                near_copy(v).wait_recv()
                far_s[at, :] = (part[m - 1, at, :] + near_r[at, :].astype(f32)).astype(bf16)
                far_copy(v).start()

            @pl.when((v >= UNITS) & (v < 2 * UNITS))
            def _():
                u = v - UNITS
                at = whole(u, unit)
                mix_copy(u).wait_recv()
                value = jnp.dot(mix_r[at, :], handed[0], preferred_element_type=f32)
                far_s[whole(v, unit), :] = (part[2, at, :] + value).astype(bf16)
                far_copy(v).start()

            @pl.when((v >= 2) & (v < UNITS + 2))
            def _():
                u = v - 2
                at = whole(u, unit)
                far_copy(u).wait_recv()
                home_s[at, :] = (part[0, at, :] + far_r[at, :].astype(f32)).astype(bf16)
                home_copy(u).start()

            return 0

        lax.fori_loop(0, 2 * UNITS + 2, step, 0)
        take_handed(1)
        part[1] = part[1] + jnp.dot(mix_r[...], handed[1], preferred_element_type=f32)

        def last(u, _):
            far_copy(UNITS + u).wait_recv()
            finish(u, part[1, whole(u, unit), :] + far_r[whole(UNITS + u, unit), :].astype(f32))
            return 0

        lax.fori_loop(0, UNITS, last, 0)

    pl.when(at_end)(ends)
    pl.when(at_mid)(mids)

    @pl.when(me < n - 1)
    def _():
        halo_copy.wait_send()

    for k in range(1, n):
        h_copy(k).wait_send()
        for q in range(1, p):
            f_copy(k, q).wait_send()
        g_copy(k).wait_send()
        for r in range(PIECES):
            c_copy(r, k).wait_send()

    @pl.when(at_end)
    def _():
        for j in range(HANDED):
            w_copy(j).wait_send()
        for u in range(UNITS):
            near_copy(u).wait_send()
            mix_copy(u).wait_send()

    @pl.when(at_mid)
    def _():
        for j in range(HANDED):
            for k in range(n):
                if k:
                    s_copy(j, k).wait_send()
                for q in range(1, p):
                    b_copy(j, k, q).wait_send()
        for u in range(UNITS):
            home_copy(u).wait_send()
        for v in range(2 * UNITS):
            far_copy(v).wait_send()

    for u in range(UNITS):
        out_copy(u).wait()


def scratch_of(n, m, p, rows, width, all_out):
    cols, out_cols = width // n, all_out // m
    f32, bf16 = jnp.float32, jnp.bfloat16
    return [
        ((3, rows, width), bf16),
        ((3, TAPS, width), f32),
        ((rows, width), f32),
        ((1, width), f32),
        ((2 * rows, 2 * rows), bf16),
        ((rows, 2 * rows), bf16),
        ((width, all_out), bf16),
        ((rows, out_cols), bf16),
        ((3, HALO, width), bf16),
        ((3, HALO + rows, cols), f32),
        ((n, rows, cols), bf16),
        ((n, rows, cols), bf16),
        ((n + 1, rows, cols), bf16),
        ((n, rows, cols), bf16),
        ((rows, width), f32),
        ((rows, width), f32),
        ((n, 2 * rows, cols), f32),
        ((n, 3, rows, cols), f32),
        ((n, 2 * rows, cols), bf16),
        ((n, rows, cols), bf16),
        ((n, rows, cols), bf16),
        ((rows, width), bf16),
        ((m, rows, out_cols), f32),
        ((rows, out_cols), bf16),
        ((rows, out_cols), bf16),
        ((rows, width), bf16),
        ((2 * rows, out_cols), bf16),
        ((2 * rows, out_cols), bf16),
        ((rows, out_cols), bf16),
        ((rows, out_cols), bf16),
        ((HANDED, width, out_cols), bf16),
    ]


def fused_local(n, m, p, projected, short_taps, long_filter, skip_gain, w_out):
    rows, width = projected.shape[1:]
    all_out = w_out.shape[1]
    both, inverse = block_tables(rows)
    anywhere = pl.BlockSpec(memory_space=pl.ANY)
    counts = [
        (7,), (UNITS,), (2,), (n,), (n,), (n, p), (n, p), (n,), (n,), (PIECES, n), (PIECES, n),
        (UNITS,), (UNITS,), (UNITS,), (UNITS,), (2 * UNITS,), (2 * UNITS,), (UNITS,), (UNITS,),
        (HANDED,), (HANDED,), (HANDED, n), (HANDED, n), (HANDED, n, p), (HANDED, n, p),
    ]
    return pl.pallas_call(
        functools.partial(operator_kernel, n, m, p),
        out_shape=jax.ShapeDtypeStruct((rows, all_out // m), jnp.bfloat16),
        in_specs=[anywhere] * 7,
        out_specs=anywhere,
        scratch_shapes=[pltpu.VMEM(*one) for one in scratch_of(n, m, p, rows, width, all_out)]
        + [pltpu.SemaphoreType.DMA(count) for count in counts],
        compiler_params=pltpu.CompilerParams(
            collective_id=0, has_side_effects=True, vmem_limit_bytes=LIMIT
        ),
    )(projected, short_taps, long_filter, skip_gain.reshape(1, width), w_out, both, inverse)


def fits_kernel(n, m, p, rows, width, all_out):
    if n < 2 or m != HANDED + 2 or width % (128 * n * p) or all_out % (128 * m):
        return False
    if rows % (16 * UNITS) or rows % STRIP or rows % (16 * PIECES):
        return False
    held = sum(
        math.prod(shape) * jnp.dtype(kind).itemsize
        for shape, kind in scratch_of(n, m, p, rows, width, all_out)
    )
    return held + 12 * 1024 * 1024 < LIMIT


def local(n, m, p, projected, short_taps, long_filter, skip_gain, w_out):
    rows, width = projected.shape[1:]
    if fits_kernel(n, m, p, rows, width, w_out.shape[1]):
        return fused_local(n, m, p, projected, short_taps, long_filter, skip_gain, w_out)
    return plain_local(projected, short_taps, long_filter, skip_gain, w_out)


def solution(mesh):
    in_specs = (
        P(None, ("dp", "ctx"), "tp"),
        P(None, None, "tp"),
        P("ctx", "tp"),
        P("tp"),
        P("tp", None),
    )
    out_specs = P(("dp", "ctx"), "tp")
    body = functools.partial(local, mesh.shape["ctx"], mesh.shape["tp"], mesh.shape["dp"])
    return jax.shard_map(body, mesh=mesh, in_specs=in_specs, out_specs=out_specs, check_vma=False)
```

```python
import functools
import math

import jax
import jax.numpy as jnp
import numpy as np
from jax import lax
from jax.experimental import pallas as pl
from jax.experimental.pallas import tpu as pltpu
from jax.sharding import PartitionSpec as P

TAPS = 7


exact_mode = lax.Precision.HIGHEST


def passed_along(block, axis, distance):
    devices = range(lax.axis_size(axis))
    route = [(i - distance, i) for i in devices if i - distance in devices]
    return lax.ppermute(block, axis, route)


def phase_table(left_index, right_index, period, sign_factor):
    turns = left_index * right_index % period
    angle = 2.0 * math.pi / period * turns.astype(jnp.float32)
    return (jnp.cos(angle), sign_factor * jnp.sin(angle))


def complex_apply(form, table_real, table_imag, data_real, data_imag):
    out_real = jnp.einsum(form, table_real, data_real, precision=exact_mode) - jnp.einsum(
        form, table_imag, data_imag, precision=exact_mode
    )
    out_imag = jnp.einsum(form, table_real, data_imag, precision=exact_mode) + jnp.einsum(
        form, table_imag, data_real, precision=exact_mode
    )
    return (out_real, out_imag)


def small_factor(length_all):
    factor = 1
    for candidate in range(1, length_all + 1):
        if candidate * candidate > length_all:
            break
        if length_all % candidate == 0:
            factor = candidate
    return factor


def local_dft(real_part, imag_part, sign_factor):
    dims_in = real_part.shape
    length_all = dims_in[-2]
    factor_one = small_factor(length_all)
    factor_two = length_all // factor_one
    leading = dims_in[:-2]
    channels = dims_in[-1]
    real_view = real_part.reshape(leading + (factor_one, factor_two, channels))
    imag_view = imag_part.reshape(leading + (factor_one, factor_two, channels))
    index_one = jnp.arange(factor_one, dtype=jnp.int32)
    index_two = jnp.arange(factor_two, dtype=jnp.int32)
    cos_one, sin_one = phase_table(index_one[:, None], index_one[None, :], factor_one, sign_factor)
    section_real, section_imag = complex_apply(
        "kn,...nmc->...kmc", cos_one, sin_one, real_view, imag_view
    )
    twist_real, twist_imag = phase_table(
        index_one[:, None], index_two[None, :], length_all, sign_factor
    )
    twist_real = twist_real[..., None]
    twist_imag = twist_imag[..., None]
    turned_real = section_real * twist_real - section_imag * twist_imag
    turned_imag = section_real * twist_imag + section_imag * twist_real
    cos_two, sin_two = phase_table(index_two[:, None], index_two[None, :], factor_two, sign_factor)
    final_real, final_imag = complex_apply(
        "dm,...kmc->...dkc", cos_two, sin_two, turned_real, turned_imag
    )
    return (final_real.reshape(dims_in), final_imag.reshape(dims_in))


def split_channels_conv(gated, long_filter):
    signals = jnp.stack([gated, long_filter])
    columns = lax.all_to_all(signals, "ctx", split_axis=2, concat_axis=1, tiled=True)
    whole_rows = columns.shape[1]
    total_len = 2 * whole_rows
    padded = jnp.concatenate([columns, jnp.zeros_like(columns)], axis=1)
    spec_real, spec_imag = local_dft(padded, jnp.zeros_like(padded), -1.0)
    prod_real = spec_real[0] * spec_real[1] - spec_imag[0] * spec_imag[1]
    prod_imag = spec_real[0] * spec_imag[1] + spec_imag[0] * spec_real[1]
    back_real, back_imag = local_dft(prod_real, prod_imag, 1.0)
    result_cols = back_real[:whole_rows] * (1.0 / total_len)
    return lax.all_to_all(result_cols, "ctx", split_axis=0, concat_axis=1, tiled=True)


def plain_local(projected, short_taps, long_filter, skip_gain, w_out):
    seq_rows = projected.shape[1]
    prior = passed_along(projected[:, seq_rows - (TAPS - 1) :, :], "ctx", 1)
    extended = jnp.concatenate([prior, projected], axis=1).astype(jnp.float32)
    featured = short_taps[:, 0, None, :] * extended[:, TAPS - 1 : TAPS - 1 + seq_rows, :]
    for tap_index in range(1, TAPS):
        featured = (
            featured
            + short_taps[:, tap_index, None, :]
            * extended[:, TAPS - 1 - tap_index : TAPS - 1 - tap_index + seq_rows, :]
        )
    query = featured[0]
    gated = featured[1] * featured[2]
    long_conv = split_channels_conv(gated, long_filter)
    mixed = (query * (long_conv + skip_gain[None, :] * gated)).astype(jnp.bfloat16)
    partial_terms = jnp.dot(mixed, w_out, preferred_element_type=jnp.float32)
    return lax.psum_scatter(
        partial_terms.astype(jnp.bfloat16), "tp", scatter_dimension=1, tiled=True
    )


HALO = 8
STRIP = 32
PIECES = 4
UNITS = 8
HANDED = 2
SIDE = 2
LIMIT = 60 * 1024 * 1024
MESH_ID = pl.DeviceIdType.MESH


def block_tables(rows):
    length = 2 * rows
    k = np.arange(rows)[:, None]
    t = np.arange(rows)[None, :]
    angle = 2.0 * np.pi / length * (k * t % length)
    real, imag = np.cos(angle), -np.sin(angle)
    imag[0] = np.where(t[0] % 2 == 0, 1.0, -1.0)
    forward = np.concatenate([real, imag], axis=0)
    sign = np.where(k % 2 == 0, 1.0, -1.0)
    both = np.concatenate([forward * np.concatenate([sign, sign], axis=0), forward], axis=1)
    weight = np.where(k == 0, 1.0, 2.0) / length
    inverse = np.concatenate([real * weight, imag * weight], axis=0).T
    as_bf16 = lambda table: jnp.asarray(np.asarray(table, np.float32), jnp.bfloat16)
    return as_bf16(both), as_bf16(inverse)


def operator_kernel(
    n, m, p, proj_hbm, taps_hbm, filt_hbm, skip_hbm, w_hbm, both_hbm, inverse_hbm, out_hbm,
    proj, taps, filt, skip, both, inverse, w, out,
    halo, ext, gsend, hsend, hbuf, gall, gated, query, gspec, kspec, zspec,
    csend, conv, mixed, part, near_s, near_r, mix_r, far_s, far_r, home_s, home_r, handed,
    load_sem, out_sem, halo_sem, h_ss, h_rs, f_ss, f_rs, g_ss, g_rs, c_ss, c_rs,
    near_ss, near_rs, mix_ss, mix_rs, far_ss, far_rs, home_ss, home_rs,
    w_ss, w_rs, s_ss, s_rs, b_ss, b_rs,
):
    me = lax.axis_index("ctx")
    z = lax.axis_index("tp")
    core = lax.axis_index("dp")
    rows, width = proj.shape[1], proj.shape[2]
    cols = width // n
    out_cols = out.shape[1]
    piece = rows // PIECES
    unit = rows // UNITS
    f32, bf16 = jnp.float32, jnp.bfloat16

    lower = 2 * z < m
    inner = jnp.where(lower, z, m - 1 - z)
    at_end = inner == 0
    at_mid = inner == 1
    pair = z + 1 - 2 * lax.rem(z, 2)
    across = m - 1 - z

    barrier = pltpu.get_barrier_semaphore()
    for k in range(1, n):
        pl.semaphore_signal(
            barrier, inc=1, device_id={"ctx": lax.rem(me + k, n)}, device_id_type=MESH_ID
        )
    for k in range(1, p):
        pl.semaphore_signal(
            barrier, inc=1, device_id={"dp": lax.rem(core + k, p)}, device_id_type=MESH_ID
        )
    pl.semaphore_signal(barrier, inc=1, device_id={"tp": pair}, device_id_type=MESH_ID)

    @pl.when(at_mid)
    def _():
        pl.semaphore_signal(barrier, inc=1, device_id={"tp": across}, device_id_type=MESH_ID)

    pairs = (
        (filt_hbm, filt), (proj_hbm, proj), (taps_hbm, taps), (both_hbm, both),
        (inverse_hbm, inverse), (skip_hbm, skip), (w_hbm, w),
    )
    loads = [pltpu.make_async_copy(a, b, load_sem.at[i]) for i, (a, b) in enumerate(pairs)]
    filt_load, proj_load, taps_load, both_load, inverse_load, skip_load, w_load = loads
    for load in (filt_load, proj_load, taps_load):
        load.start()

    filt_load.wait()
    for c in range(n):
        hsend[c] = filt[:, c * cols : (c + 1) * cols].astype(bf16)
    hbuf[0] = jnp.zeros((rows, cols), bf16)
    hbuf[me + 1] = hsend[me]
    proj_load.wait()
    for load in (both_load, inverse_load, skip_load, w_load):
        load.start()

    pl.semaphore_wait(barrier, n - 1 + p - 1 + 1 + jnp.where(at_mid, 1, 0))

    halo_copy = pltpu.make_async_remote_copy(
        proj.at[:, rows - HALO :, :], halo, halo_sem.at[0], halo_sem.at[1],
        device_id={"ctx": lax.rem(me + 1, n)}, device_id_type=MESH_ID,
    )

    @pl.when(me < n - 1)
    def _():
        halo_copy.start()

    @pl.when(me == 0)
    def _():
        halo[...] = jnp.zeros_like(halo)

    share = cols // p
    mine = pl.ds(pl.multiple_of(core * share, share), share)
    group = width // (n * p)

    def whole(index, size):
        return pl.ds(pl.multiple_of(index * size, size), size)

    def real(d):
        return jnp.where(lower, d, m - 1 - d)

    def block(d):
        return whole(real(d), out_cols)

    def h_copy(k):
        c = lax.rem(me + k, n)
        return pltpu.make_async_remote_copy(
            hsend.at[c, :, mine], hbuf.at[me + 1, :, mine], h_ss.at[k], h_rs.at[k],
            device_id={"ctx": c}, device_id_type=MESH_ID,
        )

    def f_copy(k, q):
        b = lax.rem(me + n - k, n) + 1
        return pltpu.make_async_remote_copy(
            hbuf.at[b, :, mine], hbuf.at[b, :, mine], f_ss.at[k, q], f_rs.at[k, q],
            device_id={"dp": lax.rem(core + q, p)}, device_id_type=MESH_ID,
        )

    def g_copy(k):
        c = lax.rem(me + k, n)
        return pltpu.make_async_remote_copy(
            gsend.at[c], gall.at[me], g_ss.at[k], g_rs.at[k],
            device_id={"ctx": c}, device_id_type=MESH_ID,
        )

    def c_copy(r, k):
        c = lax.rem(me + k, n)
        span = whole(r, piece)
        return pltpu.make_async_remote_copy(
            csend.at[c, span], conv.at[me, span], c_ss.at[r, k], c_rs.at[r, k],
            device_id={"ctx": c}, device_id_type=MESH_ID,
        )

    def near_copy(u):
        return pltpu.make_async_remote_copy(
            near_s.at[whole(u, unit)], near_r.at[whole(u, unit)], near_ss.at[u], near_rs.at[u],
            device_id={"tp": pair}, device_id_type=MESH_ID,
        )

    def mix_copy(u):
        return pltpu.make_async_remote_copy(
            mixed.at[whole(u, unit)], mix_r.at[whole(u, unit)], mix_ss.at[u], mix_rs.at[u],
            device_id={"tp": pair}, device_id_type=MESH_ID,
        )

    def far_copy(v):
        return pltpu.make_async_remote_copy(
            far_s.at[whole(v, unit)], far_r.at[whole(v, unit)], far_ss.at[v], far_rs.at[v],
            device_id={"tp": across}, device_id_type=MESH_ID,
        )

    def home_copy(u):
        return pltpu.make_async_remote_copy(
            home_s.at[whole(u, unit)], home_r.at[whole(u, unit)], home_ss.at[u], home_rs.at[u],
            device_id={"tp": pair}, device_id_type=MESH_ID,
        )

    beside = me + 1 - 2 * lax.rem(me, SIDE)
    above = lax.rem(me + SIDE, n)
    corner = lax.rem(beside + SIDE, n)
    plane = (me, beside, above, corner)
    half = group // 2

    def rows_of(k):
        return whole(plane[k] * p + core, group)

    def half_of(k, i):
        return whole((plane[k] * p + core) * 2 + i, half)

    def w_copy(j):
        return pltpu.make_async_remote_copy(
            w_hbm.at[rows_of(0), block(m - 2 - j)], handed.at[j, rows_of(0)],
            w_ss.at[j], w_rs.at[j], device_id={"tp": pair}, device_id_type=MESH_ID,
        )

    def s_copy(j, k, i):
        if i < 2:
            at = half_of(0, i if k == 0 else 1 - i)
        else:
            at = half_of(2, 1) if k == 0 else half_of(1, 0)
        return pltpu.make_async_remote_copy(
            handed.at[j, at], handed.at[j, at], s_ss.at[j, k, i], s_rs.at[j, k, i],
            device_id={"ctx": (beside, above)[k]}, device_id_type=MESH_ID,
        )

    def b_copy(j, k, q):
        return pltpu.make_async_remote_copy(
            handed.at[j, rows_of(k)], handed.at[j, rows_of(k)],
            b_ss.at[j, k, q], b_rs.at[j, k, q],
            device_id={"dp": lax.rem(core + q, p)}, device_id_type=MESH_ID,
        )

    def out_copy(u):
        return pltpu.make_async_copy(
            out.at[whole(u, unit)], out_hbm.at[whole(u, unit)], out_sem.at[u]
        )

    for k in range(1, n):
        h_copy(k).start()

    @pl.when(at_end)
    def _():
        for j in range(HANDED):
            w_copy(j).start()

    def features(i, start, span):
        total = None
        for j in range(TAPS):
            term = taps[i, pl.ds(j, 1), span] * ext[i, pl.ds(HALO + start - j, STRIP), :]
            total = term if total is None else total + term
        return total

    def fill_body(i, span):
        ext[i, HALO:, :] = proj[i, :, span].astype(f32)

    def fill_head(i, span):
        ext[i, :HALO, :] = halo[i, :, span].astype(f32)

    taps_load.wait()

    def gate_block(k, _):
        c = lax.rem(me + 1 + k, n)
        span = whole(c, cols)
        fill_body(1, span)
        fill_body(2, span)

        def strip(start):
            value = features(1, start, span) * features(2, start, span)
            gated[start : start + STRIP, span] = value
            gsend[c, start : start + STRIP, :] = value.astype(bf16)

        for start in reversed(range(STRIP, rows, STRIP)):
            strip(start)

        @pl.when((k == 0) & (me > 0))
        def _():
            halo_copy.wait_recv()

        fill_head(1, span)
        fill_head(2, span)
        strip(0)

        @pl.when(k < n - 1)
        def _():
            g_copy(k + 1).start()

        return 0

    lax.fori_loop(0, n, gate_block, 0)
    gall[me] = gsend[me]

    def query_block(c, _):
        span = whole(c, cols)
        fill_body(0, span)
        fill_head(0, span)
        for start in range(0, rows, STRIP):
            query[start : start + STRIP, span] = features(0, start, span)
        return 0

    for k in range(1, n):
        h_copy(k).wait_recv()
        for q in range(1, p):
            f_copy(k, q).start()

    lax.fori_loop(0, n, query_block, 0)

    for k in range(1, n):
        for q in range(1, p):
            f_copy(k, q).wait_recv()
    both_load.wait()

    first_row = lax.broadcasted_iota(jnp.int32, (rows, cols), 0) == 0

    def filter_spectrum(b, _):
        two = hbuf[pl.ds(b, 2)].reshape(2 * rows, cols)
        spec = jnp.dot(both[...], two, preferred_element_type=f32)
        re, im = spec[:rows], spec[rows:]
        kspec[b, 0] = re
        kspec[b, 1] = jnp.where(first_row, 0.0, im)
        kspec[b, 2] = jnp.where(first_row, im, re)
        return 0

    lax.fori_loop(0, n, filter_spectrum, 0)

    def signal_spectrum(k, _):
        b = lax.rem(me + n - k, n)

        @pl.when(k > 0)
        def _():
            g_copy(k).wait_recv()

        gspec[b] = jnp.dot(both[:, rows:], gall[b], preferred_element_type=f32)
        return 0

    lax.fori_loop(0, n, signal_spectrum, 0)

    def product(s, _):
        real_at = whole(s, 16)
        imag_at = pl.ds(pl.multiple_of(rows + s * 16, 16), 16)
        for lane in range(0, cols, 128):
            lanes = slice(lane, lane + 128)
            g_re = [gspec[b, real_at, lanes] for b in range(n)]
            g_im = [gspec[b, imag_at, lanes] for b in range(n)]
            k_re = [kspec[b, 0, real_at, lanes] for b in range(n)]
            k_im = [kspec[b, 1, real_at, lanes] for b in range(n)]
            k_alt = [kspec[b, 2, real_at, lanes] for b in range(n)]
            for i in range(n):
                z_re = z_im = None
                for j in range(i + 1):
                    t_re = g_re[j] * k_re[i - j] - g_im[j] * k_im[i - j]
                    t_im = g_re[j] * k_im[i - j] + g_im[j] * k_alt[i - j]
                    z_re = t_re if z_re is None else z_re + t_re
                    z_im = t_im if z_im is None else z_im + t_im
                zspec[i, real_at, lanes] = z_re.astype(bf16)
                zspec[i, imag_at, lanes] = z_im.astype(bf16)
        return 0

    lax.fori_loop(0, rows // 16, product, 0)
    inverse_load.wait()

    def back(r, _):
        span = whole(r, piece)
        for k in range(n):
            c = lax.rem(me + 1 + k, n)
            value = jnp.dot(inverse[span, :], zspec[c], preferred_element_type=f32).astype(bf16)
            if k < n - 1:
                csend[c, span, :] = value
                c_copy(r, k + 1).start()
            else:
                conv[me, span, :] = value
        return 0

    lax.fori_loop(0, PIECES, back, 0)

    def spread(j):
        w_copy(j).wait_recv()
        for i in range(2):
            for k in range(2):
                s_copy(j, k, i).start()
        for q in range(1, p):
            b_copy(j, 0, q).start()

    def relay(j):
        for k in range(2):
            s_copy(j, k, 0).wait_recv()
            s_copy(j, 1 - k, 2).start()

    def forward(j):
        for k in range(2):
            s_copy(j, k, 1).wait_recv()
            for q in range(1, p):
                b_copy(j, k + 1, q).start()

    def take(j):
        for k in range(2):
            s_copy(j, k, 2).wait_recv()
        for q in range(1, p):
            b_copy(j, n - 1, q).start()
        for k in range(n):
            for q in range(1, p):
                b_copy(j, k, q).wait_recv()

    skip_load.wait()
    w_load.wait()

    @pl.when(at_mid)
    def _():
        spread(0)

    def mix_piece(r):
        span = whole(r, piece)
        for k in range(1, n):
            c_copy(r, k).wait_recv()
        for c in range(n):
            at = slice(c * cols, (c + 1) * cols)
            mixed[span, at] = (
                query[span, at]
                * (conv[c, span, :].astype(f32) + skip[:, at] * gated[span, at])
            ).astype(bf16)
        value = jnp.dot(mixed[span, :], w[:, block(m - 1)], preferred_element_type=f32)

        @pl.when(at_end)
        def _():
            near_s[span, :] = value.astype(bf16)
            for u in range(UNITS // PIECES):
                near_copy(r * (UNITS // PIECES) + u).start()

        @pl.when(at_mid)
        def _():
            part[m - 1, span, :] = value

    def own_part(d):
        part[d] = jnp.dot(mixed[...], w[:, block(d)], preferred_element_type=f32)

    def finish(u, value):
        out[whole(u, unit), :] = value.astype(bf16)
        out_copy(u).start()

    def ends():
        def first(r, _):
            mix_piece(r)
            return 0

        lax.fori_loop(0, PIECES, first, 0)

        def give(u, _):
            mix_copy(u).start()
            return 0

        lax.fori_loop(0, UNITS, give, 0)
        own_part(0)

        def last(u, _):
            home_copy(u).wait_recv()
            at = whole(u, unit)
            finish(u, part[0, at, :] + home_r[at, :].astype(f32))
            return 0

        lax.fori_loop(0, UNITS, last, 0)

    def mids():
        def step(s, _):
            @pl.when(s < PIECES)
            def _():
                mix_piece(s)

            @pl.when(s == PIECES)
            def _():
                own_part(0)

            @pl.when(s == PIECES + 1)
            def _():
                own_part(2)

            @pl.when(s == PIECES + 2)
            def _():
                own_part(1)

            @pl.when(s == UNITS - 2)
            def _():
                relay(0)
                spread(1)

            @pl.when(s == UNITS)
            def _():
                forward(0)

            @pl.when(s == UNITS + 2)
            def _():
                take(0)

            @pl.when(s == UNITS + 4)
            def _():
                relay(1)

            v = s - 2

            @pl.when((v >= 0) & (v < UNITS))
            def _():
                at = whole(v, unit)
                near_copy(v).wait_recv()
                far_s[at, :] = (part[m - 1, at, :] + near_r[at, :].astype(f32)).astype(bf16)
                far_copy(v).start()

            @pl.when((v >= UNITS) & (v < 2 * UNITS))
            def _():
                u = v - UNITS
                at = whole(u, unit)
                mix_copy(u).wait_recv()
                value = jnp.dot(mix_r[at, :], handed[0], preferred_element_type=f32)
                far_s[whole(v, unit), :] = (part[2, at, :] + value).astype(bf16)
                far_copy(v).start()

            @pl.when((v >= 2) & (v < UNITS + 2))
            def _():
                u = v - 2
                at = whole(u, unit)
                far_copy(u).wait_recv()
                home_s[at, :] = (part[0, at, :] + far_r[at, :].astype(f32)).astype(bf16)
                home_copy(u).start()

            return 0

        lax.fori_loop(0, 2 * UNITS + 2, step, 0)
        forward(1)
        take(1)
        part[1] = part[1] + jnp.dot(mix_r[...], handed[1], preferred_element_type=f32)

        def last(u, _):
            far_copy(UNITS + u).wait_recv()
            finish(u, part[1, whole(u, unit), :] + far_r[whole(UNITS + u, unit), :].astype(f32))
            return 0

        lax.fori_loop(0, UNITS, last, 0)

    pl.when(at_end)(ends)
    pl.when(at_mid)(mids)

    @pl.when(me < n - 1)
    def _():
        halo_copy.wait_send()

    for k in range(1, n):
        h_copy(k).wait_send()
        for q in range(1, p):
            f_copy(k, q).wait_send()
        g_copy(k).wait_send()
        for r in range(PIECES):
            c_copy(r, k).wait_send()

    @pl.when(at_end)
    def _():
        for j in range(HANDED):
            w_copy(j).wait_send()
        for u in range(UNITS):
            near_copy(u).wait_send()
            mix_copy(u).wait_send()

    @pl.when(at_mid)
    def _():
        for j in range(HANDED):
            for k in range(2):
                for i in range(3):
                    s_copy(j, k, i).wait_send()
            for k in range(n):
                for q in range(1, p):
                    b_copy(j, k, q).wait_send()
        for u in range(UNITS):
            home_copy(u).wait_send()
        for v in range(2 * UNITS):
            far_copy(v).wait_send()

    for u in range(UNITS):
        out_copy(u).wait()


def scratch_of(n, m, p, rows, width, all_out):
    cols, out_cols = width // n, all_out // m
    f32, bf16 = jnp.float32, jnp.bfloat16
    return [
        ((3, rows, width), bf16),
        ((3, TAPS, width), f32),
        ((rows, width), f32),
        ((1, width), f32),
        ((2 * rows, 2 * rows), bf16),
        ((rows, 2 * rows), bf16),
        ((width, all_out), bf16),
        ((rows, out_cols), bf16),
        ((3, HALO, width), bf16),
        ((3, HALO + rows, cols), f32),
        ((n, rows, cols), bf16),
        ((n, rows, cols), bf16),
        ((n + 1, rows, cols), bf16),
        ((n, rows, cols), bf16),
        ((rows, width), f32),
        ((rows, width), f32),
        ((n, 2 * rows, cols), f32),
        ((n, 3, rows, cols), f32),
        ((n, 2 * rows, cols), bf16),
        ((n, rows, cols), bf16),
        ((n, rows, cols), bf16),
        ((rows, width), bf16),
        ((m, rows, out_cols), f32),
        ((rows, out_cols), bf16),
        ((rows, out_cols), bf16),
        ((rows, width), bf16),
        ((2 * rows, out_cols), bf16),
        ((2 * rows, out_cols), bf16),
        ((rows, out_cols), bf16),
        ((rows, out_cols), bf16),
        ((HANDED, width, out_cols), bf16),
    ]


def fused_local(n, m, p, projected, short_taps, long_filter, skip_gain, w_out):
    rows, width = projected.shape[1:]
    all_out = w_out.shape[1]
    both, inverse = block_tables(rows)
    anywhere = pl.BlockSpec(memory_space=pl.ANY)
    counts = [
        (7,), (UNITS,), (2,), (n,), (n,), (n, p), (n, p), (n,), (n,), (PIECES, n), (PIECES, n),
        (UNITS,), (UNITS,), (UNITS,), (UNITS,), (2 * UNITS,), (2 * UNITS,), (UNITS,), (UNITS,),
        (HANDED,), (HANDED,), (HANDED, 2, 3), (HANDED, 2, 3), (HANDED, n, p), (HANDED, n, p),
    ]
    return pl.pallas_call(
        functools.partial(operator_kernel, n, m, p),
        out_shape=jax.ShapeDtypeStruct((rows, all_out // m), jnp.bfloat16),
        in_specs=[anywhere] * 7,
        out_specs=anywhere,
        scratch_shapes=[pltpu.VMEM(*one) for one in scratch_of(n, m, p, rows, width, all_out)]
        + [pltpu.SemaphoreType.DMA(count) for count in counts],
        compiler_params=pltpu.CompilerParams(
            collective_id=0, has_side_effects=True, vmem_limit_bytes=LIMIT
        ),
    )(projected, short_taps, long_filter, skip_gain.reshape(1, width), w_out, both, inverse)


def fits_kernel(n, m, p, rows, width, all_out):
    if n != SIDE * SIDE or m != HANDED + 2 or width % (128 * n * p) or all_out % (128 * m):
        return False
    if rows % (16 * UNITS) or rows % STRIP or rows % (16 * PIECES):
        return False
    held = sum(
        math.prod(shape) * jnp.dtype(kind).itemsize
        for shape, kind in scratch_of(n, m, p, rows, width, all_out)
    )
    return held + 12 * 1024 * 1024 < LIMIT


def local(n, m, p, projected, short_taps, long_filter, skip_gain, w_out):
    rows, width = projected.shape[1:]
    if fits_kernel(n, m, p, rows, width, w_out.shape[1]):
        return fused_local(n, m, p, projected, short_taps, long_filter, skip_gain, w_out)
    return plain_local(projected, short_taps, long_filter, skip_gain, w_out)


def solution(mesh):
    in_specs = (
        P(None, ("dp", "ctx"), "tp"),
        P(None, None, "tp"),
        P("ctx", "tp"),
        P("tp"),
        P("tp", None),
    )
    out_specs = P(("dp", "ctx"), "tp")
    body = functools.partial(local, mesh.shape["ctx"], mesh.shape["tp"], mesh.shape["dp"])
    return jax.shard_map(body, mesh=mesh, in_specs=in_specs, out_specs=out_specs, check_vma=False)
```

```python
import functools
import math

import jax
import jax.numpy as jnp
import numpy as np
from jax import lax
from jax.experimental import pallas as pl
from jax.experimental.pallas import tpu as pltpu
from jax.sharding import PartitionSpec as P

TAPS = 7


exact_mode = lax.Precision.HIGHEST


def passed_along(block, axis, distance):
    devices = range(lax.axis_size(axis))
    route = [(i - distance, i) for i in devices if i - distance in devices]
    return lax.ppermute(block, axis, route)


def phase_table(left_index, right_index, period, sign_factor):
    turns = left_index * right_index % period
    angle = 2.0 * math.pi / period * turns.astype(jnp.float32)
    return (jnp.cos(angle), sign_factor * jnp.sin(angle))


def complex_apply(form, table_real, table_imag, data_real, data_imag):
    out_real = jnp.einsum(form, table_real, data_real, precision=exact_mode) - jnp.einsum(
        form, table_imag, data_imag, precision=exact_mode
    )
    out_imag = jnp.einsum(form, table_real, data_imag, precision=exact_mode) + jnp.einsum(
        form, table_imag, data_real, precision=exact_mode
    )
    return (out_real, out_imag)


def small_factor(length_all):
    factor = 1
    for candidate in range(1, length_all + 1):
        if candidate * candidate > length_all:
            break
        if length_all % candidate == 0:
            factor = candidate
    return factor


def local_dft(real_part, imag_part, sign_factor):
    dims_in = real_part.shape
    length_all = dims_in[-2]
    factor_one = small_factor(length_all)
    factor_two = length_all // factor_one
    leading = dims_in[:-2]
    channels = dims_in[-1]
    real_view = real_part.reshape(leading + (factor_one, factor_two, channels))
    imag_view = imag_part.reshape(leading + (factor_one, factor_two, channels))
    index_one = jnp.arange(factor_one, dtype=jnp.int32)
    index_two = jnp.arange(factor_two, dtype=jnp.int32)
    cos_one, sin_one = phase_table(index_one[:, None], index_one[None, :], factor_one, sign_factor)
    section_real, section_imag = complex_apply(
        "kn,...nmc->...kmc", cos_one, sin_one, real_view, imag_view
    )
    twist_real, twist_imag = phase_table(
        index_one[:, None], index_two[None, :], length_all, sign_factor
    )
    twist_real = twist_real[..., None]
    twist_imag = twist_imag[..., None]
    turned_real = section_real * twist_real - section_imag * twist_imag
    turned_imag = section_real * twist_imag + section_imag * twist_real
    cos_two, sin_two = phase_table(index_two[:, None], index_two[None, :], factor_two, sign_factor)
    final_real, final_imag = complex_apply(
        "dm,...kmc->...dkc", cos_two, sin_two, turned_real, turned_imag
    )
    return (final_real.reshape(dims_in), final_imag.reshape(dims_in))


def split_channels_conv(gated, long_filter):
    signals = jnp.stack([gated, long_filter])
    columns = lax.all_to_all(signals, "ctx", split_axis=2, concat_axis=1, tiled=True)
    whole_rows = columns.shape[1]
    total_len = 2 * whole_rows
    padded = jnp.concatenate([columns, jnp.zeros_like(columns)], axis=1)
    spec_real, spec_imag = local_dft(padded, jnp.zeros_like(padded), -1.0)
    prod_real = spec_real[0] * spec_real[1] - spec_imag[0] * spec_imag[1]
    prod_imag = spec_real[0] * spec_imag[1] + spec_imag[0] * spec_real[1]
    back_real, back_imag = local_dft(prod_real, prod_imag, 1.0)
    result_cols = back_real[:whole_rows] * (1.0 / total_len)
    return lax.all_to_all(result_cols, "ctx", split_axis=0, concat_axis=1, tiled=True)


def plain_local(projected, short_taps, long_filter, skip_gain, w_out):
    seq_rows = projected.shape[1]
    prior = passed_along(projected[:, seq_rows - (TAPS - 1) :, :], "ctx", 1)
    extended = jnp.concatenate([prior, projected], axis=1).astype(jnp.float32)
    featured = short_taps[:, 0, None, :] * extended[:, TAPS - 1 : TAPS - 1 + seq_rows, :]
    for tap_index in range(1, TAPS):
        featured = (
            featured
            + short_taps[:, tap_index, None, :]
            * extended[:, TAPS - 1 - tap_index : TAPS - 1 - tap_index + seq_rows, :]
        )
    query = featured[0]
    gated = featured[1] * featured[2]
    long_conv = split_channels_conv(gated, long_filter)
    mixed = (query * (long_conv + skip_gain[None, :] * gated)).astype(jnp.bfloat16)
    partial_terms = jnp.dot(mixed, w_out, preferred_element_type=jnp.float32)
    return lax.psum_scatter(
        partial_terms.astype(jnp.bfloat16), "tp", scatter_dimension=1, tiled=True
    )


HALO = 8
STRIP = 32
PIECES = 4
UNITS = 8
HANDED = 2
SIDE = 2
LIMIT = 60 * 1024 * 1024
MESH_ID = pl.DeviceIdType.MESH


def block_tables(rows):
    length = 2 * rows
    k = np.arange(rows)[:, None]
    t = np.arange(rows)[None, :]
    angle = 2.0 * np.pi / length * (k * t % length)
    real, imag = np.cos(angle), -np.sin(angle)
    imag[0] = np.where(t[0] % 2 == 0, 1.0, -1.0)
    forward = np.concatenate([real, imag], axis=0)
    sign = np.where(k % 2 == 0, 1.0, -1.0)
    both = np.concatenate([forward * np.concatenate([sign, sign], axis=0), forward], axis=1)
    weight = np.where(k == 0, 1.0, 2.0) / length
    inverse = np.concatenate([real * weight, imag * weight], axis=0).T
    as_bf16 = lambda table: jnp.asarray(np.asarray(table, np.float32), jnp.bfloat16)
    return as_bf16(both), as_bf16(inverse)


def operator_kernel(
    n, m, p, proj_hbm, taps_hbm, filt_hbm, skip_hbm, w_hbm, both_hbm, inverse_hbm, out_hbm,
    proj, taps, filt, skip, both, inverse, w, out,
    halo, ext, gsend, hsend, hbuf, gall, gated, query, gspec, kspec, zspec,
    csend, conv, mixed, part, near_s, near_r, mix_r, far_s, far_r, home_s, home_r, handed,
    load_sem, out_sem, halo_sem, h_ss, h_rs, f_ss, f_rs, g_ss, g_rs, c_ss, c_rs,
    near_ss, near_rs, mix_ss, mix_rs, far_ss, far_rs, home_ss, home_rs,
    w_ss, w_rs, x_sem, s_ss, s_rs, b_ss, b_rs,
):
    me = lax.axis_index("ctx")
    z = lax.axis_index("tp")
    core = lax.axis_index("dp")
    rows, width = proj.shape[1], proj.shape[2]
    cols = width // n
    out_cols = out.shape[1]
    piece = rows // PIECES
    unit = rows // UNITS
    f32, bf16 = jnp.float32, jnp.bfloat16

    lower = 2 * z < m
    inner = jnp.where(lower, z, m - 1 - z)
    at_end = inner == 0
    at_mid = inner == 1
    pair = z + 1 - 2 * lax.rem(z, 2)
    across = m - 1 - z

    barrier = pltpu.get_barrier_semaphore()
    for k in range(1, n):
        pl.semaphore_signal(
            barrier, inc=1, device_id={"ctx": lax.rem(me + k, n)}, device_id_type=MESH_ID
        )
    for k in range(1, p):
        pl.semaphore_signal(
            barrier, inc=1, device_id={"dp": lax.rem(core + k, p)}, device_id_type=MESH_ID
        )
    pl.semaphore_signal(barrier, inc=1, device_id={"tp": pair}, device_id_type=MESH_ID)

    @pl.when(at_mid)
    def _():
        pl.semaphore_signal(barrier, inc=1, device_id={"tp": across}, device_id_type=MESH_ID)

    pairs = (
        (filt_hbm, filt), (proj_hbm, proj), (taps_hbm, taps), (both_hbm, both),
        (inverse_hbm, inverse), (skip_hbm, skip), (w_hbm, w),
    )
    loads = [pltpu.make_async_copy(a, b, load_sem.at[i]) for i, (a, b) in enumerate(pairs)]
    filt_load, proj_load, taps_load, both_load, inverse_load, skip_load, w_load = loads
    for load in (filt_load, proj_load, taps_load):
        load.start()

    filt_load.wait()
    for c in range(n):
        hsend[c] = filt[:, c * cols : (c + 1) * cols].astype(bf16)
    hbuf[0] = jnp.zeros((rows, cols), bf16)
    hbuf[me + 1] = hsend[me]
    proj_load.wait()
    for load in (both_load, inverse_load, skip_load, w_load):
        load.start()

    pl.semaphore_wait(barrier, n - 1 + p - 1 + 1 + jnp.where(at_mid, 1, 0))

    halo_copy = pltpu.make_async_remote_copy(
        proj.at[:, rows - HALO :, :], halo, halo_sem.at[0], halo_sem.at[1],
        device_id={"ctx": lax.rem(me + 1, n)}, device_id_type=MESH_ID,
    )

    @pl.when(me < n - 1)
    def _():
        halo_copy.start()

    @pl.when(me == 0)
    def _():
        halo[...] = jnp.zeros_like(halo)

    share = cols // p
    mine = pl.ds(pl.multiple_of(core * share, share), share)
    group = width // (n * p)

    def whole(index, size):
        return pl.ds(pl.multiple_of(index * size, size), size)

    def real(d):
        return jnp.where(lower, d, m - 1 - d)

    def block(d):
        return whole(real(d), out_cols)

    def h_copy(k):
        c = lax.rem(me + k, n)
        return pltpu.make_async_remote_copy(
            hsend.at[c, :, mine], hbuf.at[me + 1, :, mine], h_ss.at[k], h_rs.at[k],
            device_id={"ctx": c}, device_id_type=MESH_ID,
        )

    def f_copy(k, q):
        b = lax.rem(me + n - k, n) + 1
        return pltpu.make_async_remote_copy(
            hbuf.at[b, :, mine], hbuf.at[b, :, mine], f_ss.at[k, q], f_rs.at[k, q],
            device_id={"dp": lax.rem(core + q, p)}, device_id_type=MESH_ID,
        )

    def g_copy(k):
        c = lax.rem(me + k, n)
        return pltpu.make_async_remote_copy(
            gsend.at[c], gall.at[me], g_ss.at[k], g_rs.at[k],
            device_id={"ctx": c}, device_id_type=MESH_ID,
        )

    def c_copy(r, k):
        c = lax.rem(me + k, n)
        span = whole(r, piece)
        return pltpu.make_async_remote_copy(
            csend.at[c, span], conv.at[me, span], c_ss.at[r, k], c_rs.at[r, k],
            device_id={"ctx": c}, device_id_type=MESH_ID,
        )

    def near_copy(u):
        return pltpu.make_async_remote_copy(
            near_s.at[whole(u, unit)], near_r.at[whole(u, unit)], near_ss.at[u], near_rs.at[u],
            device_id={"tp": pair}, device_id_type=MESH_ID,
        )

    def mix_copy(u):
        return pltpu.make_async_remote_copy(
            mixed.at[whole(u, unit)], mix_r.at[whole(u, unit)], mix_ss.at[u], mix_rs.at[u],
            device_id={"tp": pair}, device_id_type=MESH_ID,
        )

    def far_copy(v):
        return pltpu.make_async_remote_copy(
            far_s.at[whole(v, unit)], far_r.at[whole(v, unit)], far_ss.at[v], far_rs.at[v],
            device_id={"tp": across}, device_id_type=MESH_ID,
        )

    def home_copy(u):
        return pltpu.make_async_remote_copy(
            home_s.at[whole(u, unit)], home_r.at[whole(u, unit)], home_ss.at[u], home_rs.at[u],
            device_id={"tp": pair}, device_id_type=MESH_ID,
        )

    beside = me + 1 - 2 * lax.rem(me, SIDE)
    above = lax.rem(me + SIDE, n)
    corner = lax.rem(beside + SIDE, n)
    plane = (me, beside, above, corner)
    half = group // 2
    quarter = group // 4

    def rows_of(k):
        return whole(plane[k] * p + core, group)

    def half_of(k, i):
        return whole((plane[k] * p + core) * 2 + i, half)

    def last_of(j, k, i):
        if j:
            return half_of(k, i)
        return whole((plane[k] * p + core) * 4 + 3 * i, quarter)

    def x_copy():
        start = ((corner * p + core) * 4 + 1) * quarter
        at = pl.ds(pl.multiple_of(start, quarter), half)
        return pltpu.make_async_remote_copy(
            w_hbm.at[at, block(m - 2)], handed.at[0, at], x_sem.at[0], x_sem.at[1],
            device_id={"tp": pair}, device_id_type=MESH_ID,
        )

    def w_copy(j):
        return pltpu.make_async_remote_copy(
            w_hbm.at[rows_of(0), block(m - 2 - j)], handed.at[j, rows_of(0)],
            w_ss.at[j], w_rs.at[j], device_id={"tp": pair}, device_id_type=MESH_ID,
        )

    def s_copy(j, k, i):
        if i < 2:
            at = half_of(0, i if k == 0 else 1 - i)
        else:
            at = last_of(j, 2, 1) if k == 0 else last_of(j, 1, 0)
        return pltpu.make_async_remote_copy(
            handed.at[j, at], handed.at[j, at], s_ss.at[j, k, i], s_rs.at[j, k, i],
            device_id={"ctx": (beside, above)[k]}, device_id_type=MESH_ID,
        )

    middle = pl.ds(
        pl.multiple_of(((corner * p + core) * 4 + 1) * quarter, quarter), half
    )

    def b_copy(j, i, q):
        at = (
            rows_of(0), half_of(1, 0), half_of(2, 1), half_of(1, 1), half_of(2, 0),
            last_of(j, 3, 1), last_of(j, 3, 0), middle,
        )[i]
        return pltpu.make_async_remote_copy(
            handed.at[j, at], handed.at[j, at], b_ss.at[j, i, q], b_rs.at[j, i, q],
            device_id={"dp": lax.rem(core + q, p)}, device_id_type=MESH_ID,
        )

    def share_out(j, i):
        for q in range(1, p):
            b_copy(j, i, q).start()

    def out_copy(u):
        return pltpu.make_async_copy(
            out.at[whole(u, unit)], out_hbm.at[whole(u, unit)], out_sem.at[u]
        )

    for k in range(1, n):
        h_copy(k).start()

    @pl.when(at_end)
    def _():
        w_copy(0).start()
        x_copy().start()
        w_copy(1).start()

    def features(i, start, span):
        total = None
        for j in range(TAPS):
            term = taps[i, pl.ds(j, 1), span] * ext[i, pl.ds(HALO + start - j, STRIP), :]
            total = term if total is None else total + term
        return total

    def fill_body(i, span):
        ext[i, HALO:, :] = proj[i, :, span].astype(f32)

    def fill_head(i, span):
        ext[i, :HALO, :] = halo[i, :, span].astype(f32)

    taps_load.wait()

    def gate_block(k, _):
        c = lax.rem(me + 1 + k, n)
        span = whole(c, cols)
        fill_body(1, span)
        fill_body(2, span)

        def strip(start):
            value = features(1, start, span) * features(2, start, span)
            gated[start : start + STRIP, span] = value
            gsend[c, start : start + STRIP, :] = value.astype(bf16)

        for start in reversed(range(STRIP, rows, STRIP)):
            strip(start)

        @pl.when((k == 0) & (me > 0))
        def _():
            halo_copy.wait_recv()

        fill_head(1, span)
        fill_head(2, span)
        strip(0)

        @pl.when(k < n - 1)
        def _():
            g_copy(k + 1).start()

        return 0

    lax.fori_loop(0, n, gate_block, 0)
    gall[me] = gsend[me]

    def query_block(c, _):
        span = whole(c, cols)
        fill_body(0, span)
        fill_head(0, span)
        for start in range(0, rows, STRIP):
            query[start : start + STRIP, span] = features(0, start, span)
        return 0

    for k in range(1, n):
        h_copy(k).wait_recv()
        for q in range(1, p):
            f_copy(k, q).start()

    lax.fori_loop(0, n, query_block, 0)

    for k in range(1, n):
        for q in range(1, p):
            f_copy(k, q).wait_recv()
    both_load.wait()

    def begin(j):
        w_copy(j).wait_recv()
        for k in range(2):
            s_copy(j, k, 0).start()
        share_out(j, 0)

    first_row = lax.broadcasted_iota(jnp.int32, (rows, cols), 0) == 0

    def filter_spectrum(b, _):
        two = hbuf[pl.ds(b, 2)].reshape(2 * rows, cols)
        spec = jnp.dot(both[...], two, preferred_element_type=f32)
        re, im = spec[:rows], spec[rows:]
        kspec[b, 0] = re
        kspec[b, 1] = jnp.where(first_row, 0.0, im)
        kspec[b, 2] = jnp.where(first_row, im, re)
        return 0

    @pl.when(at_mid)
    def _():
        begin(0)

    lax.fori_loop(0, n, filter_spectrum, 0)

    def signal_spectrum(k, _):
        b = lax.rem(me + n - k, n)

        @pl.when(k > 0)
        def _():
            g_copy(k).wait_recv()

        gspec[b] = jnp.dot(both[:, rows:], gall[b], preferred_element_type=f32)
        return 0

    lax.fori_loop(0, n, signal_spectrum, 0)

    def product(s, _):
        real_at = whole(s, 16)
        imag_at = pl.ds(pl.multiple_of(rows + s * 16, 16), 16)
        for lane in range(0, cols, 128):
            lanes = slice(lane, lane + 128)
            g_re = [gspec[b, real_at, lanes] for b in range(n)]
            g_im = [gspec[b, imag_at, lanes] for b in range(n)]
            k_re = [kspec[b, 0, real_at, lanes] for b in range(n)]
            k_im = [kspec[b, 1, real_at, lanes] for b in range(n)]
            k_alt = [kspec[b, 2, real_at, lanes] for b in range(n)]
            for i in range(n):
                z_re = z_im = None
                for j in range(i + 1):
                    t_re = g_re[j] * k_re[i - j] - g_im[j] * k_im[i - j]
                    t_im = g_re[j] * k_im[i - j] + g_im[j] * k_alt[i - j]
                    z_re = t_re if z_re is None else z_re + t_re
                    z_im = t_im if z_im is None else z_im + t_im
                zspec[i, real_at, lanes] = z_re.astype(bf16)
                zspec[i, imag_at, lanes] = z_im.astype(bf16)
        return 0

    lax.fori_loop(0, rows // 16, product, 0)
    inverse_load.wait()

    def back(r, _):
        span = whole(r, piece)
        for k in range(n):
            c = lax.rem(me + 1 + k, n)
            value = jnp.dot(inverse[span, :], zspec[c], preferred_element_type=f32).astype(bf16)
            if k < n - 1:
                csend[c, span, :] = value
                c_copy(r, k + 1).start()
            else:
                conv[me, span, :] = value
        return 0

    lax.fori_loop(0, PIECES, back, 0)

    def spread(j):
        if j:
            begin(j)
        for k in range(2):
            s_copy(j, k, 1).start()
        if j == 0:
            x_copy().wait_recv()
            share_out(0, 7)

    def relay(j):
        for k in range(2):
            s_copy(j, k, 0).wait_recv()
            s_copy(j, 1 - k, 2).start()
            share_out(j, 1 + k)

    def forward(j):
        for k in range(2):
            s_copy(j, k, 1).wait_recv()
            share_out(j, 3 + k)

    def corner_in(j):
        for k in range(2):
            s_copy(j, k, 2).wait_recv()
            share_out(j, 5 + k)

    def settle(j):
        for i in range(7 + (j == 0)):
            for q in range(1, p):
                b_copy(j, i, q).wait_recv()

    skip_load.wait()
    w_load.wait()

    @pl.when(at_mid)
    def _():
        spread(0)

    def mix_piece(r):
        span = whole(r, piece)
        for k in range(1, n):
            c_copy(r, k).wait_recv()
        for c in range(n):
            at = slice(c * cols, (c + 1) * cols)
            mixed[span, at] = (
                query[span, at]
                * (conv[c, span, :].astype(f32) + skip[:, at] * gated[span, at])
            ).astype(bf16)
        value = jnp.dot(mixed[span, :], w[:, block(m - 1)], preferred_element_type=f32)

        @pl.when(at_end)
        def _():
            near_s[span, :] = value.astype(bf16)
            for u in range(UNITS // PIECES):
                near_copy(r * (UNITS // PIECES) + u).start()

        @pl.when(at_mid)
        def _():
            part[m - 1, span, :] = value

    def own_part(d):
        part[d] = jnp.dot(mixed[...], w[:, block(d)], preferred_element_type=f32)

    def finish(u, value):
        out[whole(u, unit), :] = value.astype(bf16)
        out_copy(u).start()

    def ends():
        def first(r, _):
            mix_piece(r)
            return 0

        lax.fori_loop(0, PIECES, first, 0)

        def give(u, _):
            mix_copy(u).start()
            return 0

        lax.fori_loop(0, UNITS, give, 0)
        own_part(0)

        def last(u, _):
            home_copy(u).wait_recv()
            at = whole(u, unit)
            finish(u, part[0, at, :] + home_r[at, :].astype(f32))
            return 0

        lax.fori_loop(0, UNITS, last, 0)

    def mids():
        def step(s, _):
            @pl.when(s == UNITS + 2)
            def _():
                settle(0)

            v = s - 2

            @pl.when((v >= 0) & (v < UNITS))
            def _():
                at = whole(v, unit)
                near_copy(v).wait_recv()
                far_s[at, :] = (part[m - 1, at, :] + near_r[at, :].astype(f32)).astype(bf16)
                far_copy(v).start()

            @pl.when((v >= UNITS) & (v < 2 * UNITS))
            def _():
                u = v - UNITS
                at = whole(u, unit)
                mix_copy(u).wait_recv()
                value = jnp.dot(mix_r[at, :], handed[0], preferred_element_type=f32)
                far_s[whole(v, unit), :] = (part[2, at, :] + value).astype(bf16)
                far_copy(v).start()

            @pl.when(s == UNITS - 6)
            def _():
                relay(0)
                spread(1)

            @pl.when(s == UNITS - 4)
            def _():
                forward(0)

            @pl.when(s == UNITS - 2)
            def _():
                corner_in(0)

            @pl.when(s == UNITS + 4)
            def _():
                relay(1)

            @pl.when(s == UNITS + 6)
            def _():
                forward(1)

            @pl.when(s == UNITS + 9)
            def _():
                corner_in(1)

            @pl.when(s < PIECES)
            def _():
                mix_piece(s)

            @pl.when(s == PIECES)
            def _():
                own_part(0)

            @pl.when(s == PIECES + 1)
            def _():
                own_part(2)

            @pl.when(s == PIECES + 2)
            def _():
                own_part(1)

            @pl.when((v >= 2) & (v < UNITS + 2))
            def _():
                u = v - 2
                at = whole(u, unit)
                far_copy(u).wait_recv()
                home_s[at, :] = (part[0, at, :] + far_r[at, :].astype(f32)).astype(bf16)
                home_copy(u).start()

            return 0

        lax.fori_loop(0, 2 * UNITS + 2, step, 0)
        settle(1)
        part[1] = part[1] + jnp.dot(mix_r[...], handed[1], preferred_element_type=f32)

        def last(u, _):
            far_copy(UNITS + u).wait_recv()
            finish(u, part[1, whole(u, unit), :] + far_r[whole(UNITS + u, unit), :].astype(f32))
            return 0

        lax.fori_loop(0, UNITS, last, 0)

    pl.when(at_end)(ends)
    pl.when(at_mid)(mids)

    @pl.when(me < n - 1)
    def _():
        halo_copy.wait_send()

    for k in range(1, n):
        h_copy(k).wait_send()
        for q in range(1, p):
            f_copy(k, q).wait_send()
        g_copy(k).wait_send()
        for r in range(PIECES):
            c_copy(r, k).wait_send()

    @pl.when(at_end)
    def _():
        for j in range(HANDED):
            w_copy(j).wait_send()
        x_copy().wait_send()
        for u in range(UNITS):
            near_copy(u).wait_send()
            mix_copy(u).wait_send()

    @pl.when(at_mid)
    def _():
        for j in range(HANDED):
            for k in range(2):
                for i in range(3):
                    s_copy(j, k, i).wait_send()
            for i in range(7 + (j == 0)):
                for q in range(1, p):
                    b_copy(j, i, q).wait_send()
        for u in range(UNITS):
            home_copy(u).wait_send()
        for v in range(2 * UNITS):
            far_copy(v).wait_send()

    for u in range(UNITS):
        out_copy(u).wait()


def scratch_of(n, m, p, rows, width, all_out):
    cols, out_cols = width // n, all_out // m
    f32, bf16 = jnp.float32, jnp.bfloat16
    return [
        ((3, rows, width), bf16),
        ((3, TAPS, width), f32),
        ((rows, width), f32),
        ((1, width), f32),
        ((2 * rows, 2 * rows), bf16),
        ((rows, 2 * rows), bf16),
        ((width, all_out), bf16),
        ((rows, out_cols), bf16),
        ((3, HALO, width), bf16),
        ((3, HALO + rows, cols), f32),
        ((n, rows, cols), bf16),
        ((n, rows, cols), bf16),
        ((n + 1, rows, cols), bf16),
        ((n, rows, cols), bf16),
        ((rows, width), f32),
        ((rows, width), f32),
        ((n, 2 * rows, cols), f32),
        ((n, 3, rows, cols), f32),
        ((n, 2 * rows, cols), bf16),
        ((n, rows, cols), bf16),
        ((n, rows, cols), bf16),
        ((rows, width), bf16),
        ((m, rows, out_cols), f32),
        ((rows, out_cols), bf16),
        ((rows, out_cols), bf16),
        ((rows, width), bf16),
        ((2 * rows, out_cols), bf16),
        ((2 * rows, out_cols), bf16),
        ((rows, out_cols), bf16),
        ((rows, out_cols), bf16),
        ((HANDED, width, out_cols), bf16),
    ]


def fused_local(n, m, p, projected, short_taps, long_filter, skip_gain, w_out):
    rows, width = projected.shape[1:]
    all_out = w_out.shape[1]
    both, inverse = block_tables(rows)
    anywhere = pl.BlockSpec(memory_space=pl.ANY)
    counts = [
        (7,), (UNITS,), (2,), (n,), (n,), (n, p), (n, p), (n,), (n,), (PIECES, n), (PIECES, n),
        (UNITS,), (UNITS,), (UNITS,), (UNITS,), (2 * UNITS,), (2 * UNITS,), (UNITS,), (UNITS,),
        (HANDED,), (HANDED,), (2,), (HANDED, 2, 3), (HANDED, 2, 3), (HANDED, 8, p), (HANDED, 8, p),
    ]
    return pl.pallas_call(
        functools.partial(operator_kernel, n, m, p),
        out_shape=jax.ShapeDtypeStruct((rows, all_out // m), jnp.bfloat16),
        in_specs=[anywhere] * 7,
        out_specs=anywhere,
        scratch_shapes=[pltpu.VMEM(*one) for one in scratch_of(n, m, p, rows, width, all_out)]
        + [pltpu.SemaphoreType.DMA(count) for count in counts],
        compiler_params=pltpu.CompilerParams(
            collective_id=0, has_side_effects=True, vmem_limit_bytes=LIMIT
        ),
    )(projected, short_taps, long_filter, skip_gain.reshape(1, width), w_out, both, inverse)


def fits_kernel(n, m, p, rows, width, all_out):
    if n != SIDE * SIDE or m != HANDED + 2 or width % (128 * n * p) or all_out % (128 * m):
        return False
    if rows % (16 * UNITS) or rows % STRIP or rows % (16 * PIECES):
        return False
    held = sum(
        math.prod(shape) * jnp.dtype(kind).itemsize
        for shape, kind in scratch_of(n, m, p, rows, width, all_out)
    )
    return held + 12 * 1024 * 1024 < LIMIT


def local(n, m, p, projected, short_taps, long_filter, skip_gain, w_out):
    rows, width = projected.shape[1:]
    if fits_kernel(n, m, p, rows, width, w_out.shape[1]):
        return fused_local(n, m, p, projected, short_taps, long_filter, skip_gain, w_out)
    return plain_local(projected, short_taps, long_filter, skip_gain, w_out)


def solution(mesh):
    in_specs = (
        P(None, ("dp", "ctx"), "tp"),
        P(None, None, "tp"),
        P("ctx", "tp"),
        P("tp"),
        P("tp", None),
    )
    out_specs = P(("dp", "ctx"), "tp")
    body = functools.partial(local, mesh.shape["ctx"], mesh.shape["tp"], mesh.shape["dp"])
    return jax.shard_map(body, mesh=mesh, in_specs=in_specs, out_specs=out_specs, check_vma=False)
```

```python
import functools
import math

import jax
import jax.numpy as jnp
import numpy as np
from jax import lax
from jax.experimental import pallas as pl
from jax.experimental.pallas import tpu as pltpu
from jax.sharding import PartitionSpec as P

TAPS = 7


exact_mode = lax.Precision.HIGHEST


def passed_along(block, axis, distance):
    devices = range(lax.axis_size(axis))
    route = [(i - distance, i) for i in devices if i - distance in devices]
    return lax.ppermute(block, axis, route)


def phase_table(left_index, right_index, period, sign_factor):
    turns = left_index * right_index % period
    angle = 2.0 * math.pi / period * turns.astype(jnp.float32)
    return (jnp.cos(angle), sign_factor * jnp.sin(angle))


def complex_apply(form, table_real, table_imag, data_real, data_imag):
    out_real = jnp.einsum(form, table_real, data_real, precision=exact_mode) - jnp.einsum(
        form, table_imag, data_imag, precision=exact_mode
    )
    out_imag = jnp.einsum(form, table_real, data_imag, precision=exact_mode) + jnp.einsum(
        form, table_imag, data_real, precision=exact_mode
    )
    return (out_real, out_imag)


def small_factor(length_all):
    factor = 1
    for candidate in range(1, length_all + 1):
        if candidate * candidate > length_all:
            break
        if length_all % candidate == 0:
            factor = candidate
    return factor


def local_dft(real_part, imag_part, sign_factor):
    dims_in = real_part.shape
    length_all = dims_in[-2]
    factor_one = small_factor(length_all)
    factor_two = length_all // factor_one
    leading = dims_in[:-2]
    channels = dims_in[-1]
    real_view = real_part.reshape(leading + (factor_one, factor_two, channels))
    imag_view = imag_part.reshape(leading + (factor_one, factor_two, channels))
    index_one = jnp.arange(factor_one, dtype=jnp.int32)
    index_two = jnp.arange(factor_two, dtype=jnp.int32)
    cos_one, sin_one = phase_table(index_one[:, None], index_one[None, :], factor_one, sign_factor)
    section_real, section_imag = complex_apply(
        "kn,...nmc->...kmc", cos_one, sin_one, real_view, imag_view
    )
    twist_real, twist_imag = phase_table(
        index_one[:, None], index_two[None, :], length_all, sign_factor
    )
    twist_real = twist_real[..., None]
    twist_imag = twist_imag[..., None]
    turned_real = section_real * twist_real - section_imag * twist_imag
    turned_imag = section_real * twist_imag + section_imag * twist_real
    cos_two, sin_two = phase_table(index_two[:, None], index_two[None, :], factor_two, sign_factor)
    final_real, final_imag = complex_apply(
        "dm,...kmc->...dkc", cos_two, sin_two, turned_real, turned_imag
    )
    return (final_real.reshape(dims_in), final_imag.reshape(dims_in))


def split_channels_conv(gated, long_filter):
    signals = jnp.stack([gated, long_filter])
    columns = lax.all_to_all(signals, "ctx", split_axis=2, concat_axis=1, tiled=True)
    whole_rows = columns.shape[1]
    total_len = 2 * whole_rows
    padded = jnp.concatenate([columns, jnp.zeros_like(columns)], axis=1)
    spec_real, spec_imag = local_dft(padded, jnp.zeros_like(padded), -1.0)
    prod_real = spec_real[0] * spec_real[1] - spec_imag[0] * spec_imag[1]
    prod_imag = spec_real[0] * spec_imag[1] + spec_imag[0] * spec_real[1]
    back_real, back_imag = local_dft(prod_real, prod_imag, 1.0)
    result_cols = back_real[:whole_rows] * (1.0 / total_len)
    return lax.all_to_all(result_cols, "ctx", split_axis=0, concat_axis=1, tiled=True)


def plain_local(projected, short_taps, long_filter, skip_gain, w_out):
    seq_rows = projected.shape[1]
    prior = passed_along(projected[:, seq_rows - (TAPS - 1) :, :], "ctx", 1)
    extended = jnp.concatenate([prior, projected], axis=1).astype(jnp.float32)
    featured = short_taps[:, 0, None, :] * extended[:, TAPS - 1 : TAPS - 1 + seq_rows, :]
    for tap_index in range(1, TAPS):
        featured = (
            featured
            + short_taps[:, tap_index, None, :]
            * extended[:, TAPS - 1 - tap_index : TAPS - 1 - tap_index + seq_rows, :]
        )
    query = featured[0]
    gated = featured[1] * featured[2]
    long_conv = split_channels_conv(gated, long_filter)
    mixed = (query * (long_conv + skip_gain[None, :] * gated)).astype(jnp.bfloat16)
    partial_terms = jnp.dot(mixed, w_out, preferred_element_type=jnp.float32)
    return lax.psum_scatter(
        partial_terms.astype(jnp.bfloat16), "tp", scatter_dimension=1, tiled=True
    )


HALO = 8
STRIP = 32
PIECES = 4
UNITS = 8
HANDED = 2
SIDE = 2
LIMIT = 60 * 1024 * 1024
MESH_ID = pl.DeviceIdType.MESH


def block_tables(rows):
    length = 2 * rows
    k = np.arange(rows)[:, None]
    t = np.arange(rows)[None, :]
    angle = 2.0 * np.pi / length * (k * t % length)
    real, imag = np.cos(angle), -np.sin(angle)
    imag[0] = np.where(t[0] % 2 == 0, 1.0, -1.0)
    forward = np.concatenate([real, imag], axis=0)
    sign = np.where(k % 2 == 0, 1.0, -1.0)
    both = np.concatenate([forward * np.concatenate([sign, sign], axis=0), forward], axis=1)
    weight = np.where(k == 0, 1.0, 2.0) / length
    inverse = np.concatenate([real * weight, imag * weight], axis=0).T
    as_bf16 = lambda table: jnp.asarray(np.asarray(table, np.float32), jnp.bfloat16)
    return as_bf16(both), as_bf16(inverse)


def operator_kernel(
    n, m, p, proj_hbm, taps_hbm, filt_hbm, skip_hbm, w_hbm, both_hbm, inverse_hbm,
    own_hbm, got_hbm,
    proj, taps, filt, skip, both, inverse, w,
    halo, ext, gsend, hsend, hbuf, gall, gated, query, gspec, kspec, zspec,
    csend, conv, mixed, part, near_s, near_r, mix_r, far_s, far_r, home_s, handed,
    load_sem, out_sem, halo_sem, h_ss, h_rs, f_ss, f_rs, g_ss, g_rs, c_ss, c_rs,
    near_ss, near_rs, mix_ss, mix_rs, far_ss, far_rs, home_ss, home_rs,
    w_ss, w_rs, x_sem, s_ss, s_rs, b_ss, b_rs,
):
    me = lax.axis_index("ctx")
    z = lax.axis_index("tp")
    core = lax.axis_index("dp")
    rows, width = proj.shape[1], proj.shape[2]
    cols = width // n
    out_cols = own_hbm.shape[1]
    piece = rows // PIECES
    unit = rows // UNITS
    f32, bf16 = jnp.float32, jnp.bfloat16

    lower = 2 * z < m
    inner = jnp.where(lower, z, m - 1 - z)
    at_end = inner == 0
    at_mid = inner == 1
    pair = z + 1 - 2 * lax.rem(z, 2)
    across = m - 1 - z

    barrier = pltpu.get_barrier_semaphore()
    for k in range(1, n):
        pl.semaphore_signal(
            barrier, inc=1, device_id={"ctx": lax.rem(me + k, n)}, device_id_type=MESH_ID
        )
    for k in range(1, p):
        pl.semaphore_signal(
            barrier, inc=1, device_id={"dp": lax.rem(core + k, p)}, device_id_type=MESH_ID
        )
    pl.semaphore_signal(barrier, inc=1, device_id={"tp": pair}, device_id_type=MESH_ID)

    @pl.when(at_mid)
    def _():
        pl.semaphore_signal(barrier, inc=1, device_id={"tp": across}, device_id_type=MESH_ID)

    pairs = (
        (filt_hbm, filt), (proj_hbm, proj), (taps_hbm, taps), (both_hbm, both),
        (inverse_hbm, inverse), (skip_hbm, skip), (w_hbm, w),
    )
    loads = [pltpu.make_async_copy(a, b, load_sem.at[i]) for i, (a, b) in enumerate(pairs)]
    filt_load, proj_load, taps_load, both_load, inverse_load, skip_load, w_load = loads
    for load in (filt_load, proj_load, taps_load):
        load.start()

    filt_load.wait()
    for c in range(n):
        hsend[c] = filt[:, c * cols : (c + 1) * cols].astype(bf16)
    hbuf[0] = jnp.zeros((rows, cols), bf16)
    hbuf[me + 1] = hsend[me]
    proj_load.wait()
    for load in (both_load, inverse_load, skip_load, w_load):
        load.start()

    pl.semaphore_wait(barrier, n - 1 + p - 1 + 1 + jnp.where(at_mid, 1, 0))

    halo_copy = pltpu.make_async_remote_copy(
        proj.at[:, rows - HALO :, :], halo, halo_sem.at[0], halo_sem.at[1],
        device_id={"ctx": lax.rem(me + 1, n)}, device_id_type=MESH_ID,
    )

    @pl.when(me < n - 1)
    def _():
        halo_copy.start()

    @pl.when(me == 0)
    def _():
        halo[...] = jnp.zeros_like(halo)

    share = cols // p
    mine = pl.ds(pl.multiple_of(core * share, share), share)
    group = width // (n * p)

    def whole(index, size):
        return pl.ds(pl.multiple_of(index * size, size), size)

    def real(d):
        return jnp.where(lower, d, m - 1 - d)

    def block(d):
        return whole(real(d), out_cols)

    def h_copy(k):
        c = lax.rem(me + k, n)
        return pltpu.make_async_remote_copy(
            hsend.at[c, :, mine], hbuf.at[me + 1, :, mine], h_ss.at[k], h_rs.at[k],
            device_id={"ctx": c}, device_id_type=MESH_ID,
        )

    def f_copy(k, q):
        b = lax.rem(me + n - k, n) + 1
        return pltpu.make_async_remote_copy(
            hbuf.at[b, :, mine], hbuf.at[b, :, mine], f_ss.at[k, q], f_rs.at[k, q],
            device_id={"dp": lax.rem(core + q, p)}, device_id_type=MESH_ID,
        )

    def g_copy(k):
        c = lax.rem(me + k, n)
        return pltpu.make_async_remote_copy(
            gsend.at[c], gall.at[me], g_ss.at[k], g_rs.at[k],
            device_id={"ctx": c}, device_id_type=MESH_ID,
        )

    def c_copy(r, k):
        c = lax.rem(me + k, n)
        span = whole(r, piece)
        return pltpu.make_async_remote_copy(
            csend.at[c, span], conv.at[me, span], c_ss.at[r, k], c_rs.at[r, k],
            device_id={"ctx": c}, device_id_type=MESH_ID,
        )

    def near_copy(u):
        return pltpu.make_async_remote_copy(
            near_s.at[whole(u, unit)], near_r.at[whole(u, unit)], near_ss.at[u], near_rs.at[u],
            device_id={"tp": pair}, device_id_type=MESH_ID,
        )

    def mix_copy(u):
        return pltpu.make_async_remote_copy(
            mixed.at[whole(u, unit)], mix_r.at[whole(u, unit)], mix_ss.at[u], mix_rs.at[u],
            device_id={"tp": pair}, device_id_type=MESH_ID,
        )

    def far_copy(v):
        return pltpu.make_async_remote_copy(
            far_s.at[whole(v, unit)], far_r.at[whole(v, unit)], far_ss.at[v], far_rs.at[v],
            device_id={"tp": across}, device_id_type=MESH_ID,
        )

    def got_copy(u):
        v = UNITS + u
        return pltpu.make_async_remote_copy(
            far_s.at[whole(v, unit)], got_hbm.at[whole(u, unit)], far_ss.at[v], far_rs.at[v],
            device_id={"tp": across}, device_id_type=MESH_ID,
        )

    def home_copy(u):
        return pltpu.make_async_remote_copy(
            home_s.at[whole(u, unit)], got_hbm.at[whole(u, unit)], home_ss.at[u], home_rs.at[u],
            device_id={"tp": pair}, device_id_type=MESH_ID,
        )

    beside = me + 1 - 2 * lax.rem(me, SIDE)
    above = lax.rem(me + SIDE, n)
    corner = lax.rem(beside + SIDE, n)
    plane = (me, beside, above, corner)
    half = group // 2
    quarter = group // 4

    def rows_of(k):
        return whole(plane[k] * p + core, group)

    def half_of(k, i):
        return whole((plane[k] * p + core) * 2 + i, half)

    def last_of(j, k, i):
        if j:
            return half_of(k, i)
        return whole((plane[k] * p + core) * 4 + 3 * i, quarter)

    def x_copy():
        start = ((corner * p + core) * 4 + 1) * quarter
        at = pl.ds(pl.multiple_of(start, quarter), half)
        return pltpu.make_async_remote_copy(
            w_hbm.at[at, block(m - 2)], handed.at[0, at], x_sem.at[0], x_sem.at[1],
            device_id={"tp": pair}, device_id_type=MESH_ID,
        )

    def w_copy(j):
        return pltpu.make_async_remote_copy(
            w_hbm.at[rows_of(0), block(m - 2 - j)], handed.at[j, rows_of(0)],
            w_ss.at[j], w_rs.at[j], device_id={"tp": pair}, device_id_type=MESH_ID,
        )

    def s_copy(j, k, i):
        if i < 2:
            at = half_of(0, i if k == 0 else 1 - i)
        else:
            at = last_of(j, 2, 1) if k == 0 else last_of(j, 1, 0)
        return pltpu.make_async_remote_copy(
            handed.at[j, at], handed.at[j, at], s_ss.at[j, k, i], s_rs.at[j, k, i],
            device_id={"ctx": (beside, above)[k]}, device_id_type=MESH_ID,
        )

    middle = pl.ds(
        pl.multiple_of(((corner * p + core) * 4 + 1) * quarter, quarter), half
    )

    def b_copy(j, i, q):
        at = (
            rows_of(0), half_of(1, 0), half_of(2, 1), half_of(1, 1), half_of(2, 0),
            last_of(j, 3, 1), last_of(j, 3, 0), middle,
        )[i]
        return pltpu.make_async_remote_copy(
            handed.at[j, at], handed.at[j, at], b_ss.at[j, i, q], b_rs.at[j, i, q],
            device_id={"dp": lax.rem(core + q, p)}, device_id_type=MESH_ID,
        )

    def share_out(j, i):
        for q in range(1, p):
            b_copy(j, i, q).start()

    def own_copy(d):
        return pltpu.make_async_copy(part.at[d], own_hbm, out_sem)

    for k in range(1, n):
        h_copy(k).start()

    @pl.when(at_end)
    def _():
        w_copy(0).start()
        x_copy().start()
        w_copy(1).start()

    def features(i, start, span):
        total = None
        for j in range(TAPS):
            term = taps[i, pl.ds(j, 1), span] * ext[i, pl.ds(HALO + start - j, STRIP), :]
            total = term if total is None else total + term
        return total

    def fill_body(i, span):
        ext[i, HALO:, :] = proj[i, :, span].astype(f32)

    def fill_head(i, span):
        ext[i, :HALO, :] = halo[i, :, span].astype(f32)

    taps_load.wait()

    def gate_block(k, _):
        c = lax.rem(me + 1 + k, n)
        span = whole(c, cols)
        fill_body(1, span)
        fill_body(2, span)

        def strip(start):
            value = features(1, start, span) * features(2, start, span)
            gated[start : start + STRIP, span] = value
            gsend[c, start : start + STRIP, :] = value.astype(bf16)

        for start in reversed(range(STRIP, rows, STRIP)):
            strip(start)

        @pl.when((k == 0) & (me > 0))
        def _():
            halo_copy.wait_recv()

        fill_head(1, span)
        fill_head(2, span)
        strip(0)

        @pl.when(k < n - 1)
        def _():
            g_copy(k + 1).start()

        return 0

    lax.fori_loop(0, n, gate_block, 0)
    gall[me] = gsend[me]

    def query_block(c, _):
        span = whole(c, cols)
        fill_body(0, span)
        fill_head(0, span)
        for start in range(0, rows, STRIP):
            query[start : start + STRIP, span] = features(0, start, span)
        return 0

    for k in range(1, n):
        h_copy(k).wait_recv()
        for q in range(1, p):
            f_copy(k, q).start()

    lax.fori_loop(0, n, query_block, 0)

    for k in range(1, n):
        for q in range(1, p):
            f_copy(k, q).wait_recv()
    both_load.wait()

    def begin(j):
        w_copy(j).wait_recv()
        for k in range(2):
            s_copy(j, k, 0).start()
        share_out(j, 0)

    first_row = lax.broadcasted_iota(jnp.int32, (rows, cols), 0) == 0

    def filter_spectrum(b, _):
        two = hbuf[pl.ds(b, 2)].reshape(2 * rows, cols)
        spec = jnp.dot(both[...], two, preferred_element_type=f32)
        re, im = spec[:rows], spec[rows:]
        kspec[b, 0] = re
        kspec[b, 1] = jnp.where(first_row, 0.0, im)
        kspec[b, 2] = jnp.where(first_row, im, re)
        return 0

    @pl.when(at_mid)
    def _():
        begin(0)

    lax.fori_loop(0, n, filter_spectrum, 0, unroll=True)

    def signal_spectrum(k, _):
        b = lax.rem(me + n - k, n)

        @pl.when(k > 0)
        def _():
            g_copy(k).wait_recv()

        gspec[b] = jnp.dot(both[:, rows:], gall[b], preferred_element_type=f32)
        return 0

    lax.fori_loop(0, n, signal_spectrum, 0)

    def product(s, _):
        real_at = whole(s, 16)
        imag_at = pl.ds(pl.multiple_of(rows + s * 16, 16), 16)
        for lane in range(0, cols, 128):
            lanes = slice(lane, lane + 128)
            g_re = [gspec[b, real_at, lanes] for b in range(n)]
            g_im = [gspec[b, imag_at, lanes] for b in range(n)]
            k_re = [kspec[b, 0, real_at, lanes] for b in range(n)]
            k_im = [kspec[b, 1, real_at, lanes] for b in range(n)]
            k_alt = [kspec[b, 2, real_at, lanes] for b in range(n)]
            for i in range(n):
                z_re = z_im = None
                for j in range(i + 1):
                    t_re = g_re[j] * k_re[i - j] - g_im[j] * k_im[i - j]
                    t_im = g_re[j] * k_im[i - j] + g_im[j] * k_alt[i - j]
                    z_re = t_re if z_re is None else z_re + t_re
                    z_im = t_im if z_im is None else z_im + t_im
                zspec[i, real_at, lanes] = z_re.astype(bf16)
                zspec[i, imag_at, lanes] = z_im.astype(bf16)
        return 0

    lax.fori_loop(0, rows // 16, product, 0, unroll=4)
    inverse_load.wait()

    def back(r, _):
        span = whole(r, piece)
        for k in range(n):
            c = lax.rem(me + 1 + k, n)
            value = jnp.dot(inverse[span, :], zspec[c], preferred_element_type=f32).astype(bf16)
            if k < n - 1:
                csend[c, span, :] = value
                c_copy(r, k + 1).start()
            else:
                conv[me, span, :] = value
        return 0

    lax.fori_loop(0, PIECES, back, 0)

    def spread(j):
        if j:
            begin(j)
        for k in range(2):
            s_copy(j, k, 1).start()
        if j == 0:
            x_copy().wait_recv()
            share_out(0, 7)

    def relay(j):
        for k in range(2):
            s_copy(j, k, 0).wait_recv()
            s_copy(j, 1 - k, 2).start()
            share_out(j, 1 + k)

    def forward(j):
        for k in range(2):
            s_copy(j, k, 1).wait_recv()
            share_out(j, 3 + k)

    def corner_in(j):
        for k in range(2):
            s_copy(j, k, 2).wait_recv()
            share_out(j, 5 + k)

    def settle(j):
        for i in range(7 + (j == 0)):
            for q in range(1, p):
                b_copy(j, i, q).wait_recv()

    skip_load.wait()
    w_load.wait()

    @pl.when(at_mid)
    def _():
        spread(0)

    def mix_piece(r):
        span = whole(r, piece)
        for k in range(1, n):
            c_copy(r, k).wait_recv()
        for c in range(n):
            at = slice(c * cols, (c + 1) * cols)
            mixed[span, at] = (
                query[span, at]
                * (conv[c, span, :].astype(f32) + skip[:, at] * gated[span, at])
            ).astype(bf16)
        value = jnp.dot(mixed[span, :], w[:, block(m - 1)], preferred_element_type=f32)

        @pl.when(at_end)
        def _():
            near_s[span, :] = value.astype(bf16)
            for u in range(UNITS // PIECES):
                near_copy(r * (UNITS // PIECES) + u).start()

        @pl.when(at_mid)
        def _():
            part[m - 1, span, :] = value

    def own_part(d):
        part[d] = jnp.dot(mixed[...], w[:, block(d)], preferred_element_type=f32)

    def ends():
        def first(r, _):
            mix_piece(r)
            return 0

        lax.fori_loop(0, PIECES, first, 0)

        def give(u, _):
            mix_copy(u).start()
            return 0

        lax.fori_loop(0, UNITS, give, 0)
        own_part(0)
        own_copy(0).start()

        def last(u, _):
            home_copy(u).wait_recv()
            return 0

        lax.fori_loop(0, UNITS, last, 0)
        own_copy(0).wait()

    def mids():
        def step(s, _):
            @pl.when(s == UNITS + 2)
            def _():
                settle(0)

            v = s - 2

            @pl.when((v >= 0) & (v < UNITS))
            def _():
                at = whole(v, unit)
                near_copy(v).wait_recv()
                far_s[at, :] = (part[m - 1, at, :] + near_r[at, :].astype(f32)).astype(bf16)
                far_copy(v).start()

            @pl.when((v >= UNITS) & (v < 2 * UNITS))
            def _():
                u = v - UNITS
                at = whole(u, unit)
                mix_copy(u).wait_recv()
                value = jnp.dot(mix_r[at, :], handed[0], preferred_element_type=f32)
                far_s[whole(v, unit), :] = (part[2, at, :] + value).astype(bf16)
                got_copy(u).start()

            @pl.when(s == UNITS - 6)
            def _():
                relay(0)
                spread(1)

            @pl.when(s == UNITS - 4)
            def _():
                forward(0)

            @pl.when(s == UNITS - 2)
            def _():
                corner_in(0)

            @pl.when(s == UNITS + 4)
            def _():
                relay(1)

            @pl.when(s == UNITS + 6)
            def _():
                forward(1)

            @pl.when(s == UNITS + 9)
            def _():
                corner_in(1)

            @pl.when(s < PIECES)
            def _():
                mix_piece(s)

            @pl.when(s == PIECES + 1)
            def _():
                own_part(2)

            @pl.when(s == PIECES + 2)
            def _():
                own_part(1)

            @pl.when(s == PIECES)
            def _():
                own_part(0)

            @pl.when((v >= 3) & (v < UNITS + 3))
            def _():
                u = v - 3
                at = whole(u, unit)
                far_copy(u).wait_recv()
                home_s[at, :] = (part[0, at, :] + far_r[at, :].astype(f32)).astype(bf16)
                home_copy(u).start()

            return 0

        lax.fori_loop(0, 2 * UNITS + 2, step, 0)
        settle(1)
        part[1] = part[1] + jnp.dot(mix_r[...], handed[1], preferred_element_type=f32)

        own_copy(1).start()

        def last(u, _):
            got_copy(u).wait_recv()
            return 0

        lax.fori_loop(0, UNITS, last, 0)
        own_copy(1).wait()

    pl.when(at_end)(ends)
    pl.when(at_mid)(mids)

    @pl.when(me < n - 1)
    def _():
        halo_copy.wait_send()

    for k in range(1, n):
        h_copy(k).wait_send()
        for q in range(1, p):
            f_copy(k, q).wait_send()
        g_copy(k).wait_send()
        for r in range(PIECES):
            c_copy(r, k).wait_send()

    @pl.when(at_end)
    def _():
        for j in range(HANDED):
            w_copy(j).wait_send()
        x_copy().wait_send()
        for u in range(UNITS):
            near_copy(u).wait_send()
            mix_copy(u).wait_send()

    @pl.when(at_mid)
    def _():
        for j in range(HANDED):
            for k in range(2):
                for i in range(3):
                    s_copy(j, k, i).wait_send()
            for i in range(7 + (j == 0)):
                for q in range(1, p):
                    b_copy(j, i, q).wait_send()
        for u in range(UNITS):
            home_copy(u).wait_send()
        for u in range(UNITS):
            far_copy(u).wait_send()
            got_copy(u).wait_send()


def scratch_of(n, m, p, rows, width, all_out):
    cols, out_cols = width // n, all_out // m
    f32, bf16 = jnp.float32, jnp.bfloat16
    return [
        ((3, rows, width), bf16),
        ((3, TAPS, width), f32),
        ((rows, width), f32),
        ((1, width), f32),
        ((2 * rows, 2 * rows), bf16),
        ((rows, 2 * rows), bf16),
        ((width, all_out), bf16),
        ((3, HALO, width), bf16),
        ((3, HALO + rows, cols), f32),
        ((n, rows, cols), bf16),
        ((n, rows, cols), bf16),
        ((n + 1, rows, cols), bf16),
        ((n, rows, cols), bf16),
        ((rows, width), f32),
        ((rows, width), f32),
        ((n, 2 * rows, cols), f32),
        ((n, 3, rows, cols), f32),
        ((n, 2 * rows, cols), bf16),
        ((n, rows, cols), bf16),
        ((n, rows, cols), bf16),
        ((rows, width), bf16),
        ((m, rows, out_cols), f32),
        ((rows, out_cols), bf16),
        ((rows, out_cols), bf16),
        ((rows, width), bf16),
        ((2 * rows, out_cols), bf16),
        ((rows, out_cols), bf16),
        ((rows, out_cols), bf16),
        ((HANDED, width, out_cols), bf16),
    ]


def fused_local(n, m, p, projected, short_taps, long_filter, skip_gain, w_out):
    rows, width = projected.shape[1:]
    all_out = w_out.shape[1]
    both, inverse = block_tables(rows)
    anywhere = pl.BlockSpec(memory_space=pl.ANY)
    counts = [
        (7,), (), (2,), (n,), (n,), (n, p), (n, p), (n,), (n,), (PIECES, n), (PIECES, n),
        (UNITS,), (UNITS,), (UNITS,), (UNITS,), (2 * UNITS,), (2 * UNITS,), (UNITS,), (UNITS,),
        (HANDED,), (HANDED,), (2,), (HANDED, 2, 3), (HANDED, 2, 3), (HANDED, 8, p), (HANDED, 8, p),
    ]
    shape = (rows, all_out // m)
    own, got = pl.pallas_call(
        functools.partial(operator_kernel, n, m, p),
        out_shape=(
            jax.ShapeDtypeStruct(shape, jnp.float32),
            jax.ShapeDtypeStruct(shape, jnp.bfloat16),
        ),
        in_specs=[anywhere] * 7,
        out_specs=(anywhere, anywhere),
        scratch_shapes=[pltpu.VMEM(*one) for one in scratch_of(n, m, p, rows, width, all_out)]
        + [pltpu.SemaphoreType.DMA(count) for count in counts],
        compiler_params=pltpu.CompilerParams(
            collective_id=0, has_side_effects=True, vmem_limit_bytes=LIMIT
        ),
    )(projected, short_taps, long_filter, skip_gain.reshape(1, width), w_out, both, inverse)
    return (own + got.astype(jnp.float32)).astype(jnp.bfloat16)


def fits_kernel(n, m, p, rows, width, all_out):
    if n != SIDE * SIDE or m != HANDED + 2 or width % (128 * n * p) or all_out % (128 * m):
        return False
    if rows % (16 * UNITS) or rows % STRIP or rows % (16 * PIECES):
        return False
    held = sum(
        math.prod(shape) * jnp.dtype(kind).itemsize
        for shape, kind in scratch_of(n, m, p, rows, width, all_out)
    )
    return held + 12 * 1024 * 1024 < LIMIT


def local(n, m, p, projected, short_taps, long_filter, skip_gain, w_out):
    rows, width = projected.shape[1:]
    if fits_kernel(n, m, p, rows, width, w_out.shape[1]):
        return fused_local(n, m, p, projected, short_taps, long_filter, skip_gain, w_out)
    return plain_local(projected, short_taps, long_filter, skip_gain, w_out)


def solution(mesh):
    in_specs = (
        P(None, ("dp", "ctx"), "tp"),
        P(None, None, "tp"),
        P("ctx", "tp"),
        P("tp"),
        P("tp", None),
    )
    out_specs = P(("dp", "ctx"), "tp")
    body = functools.partial(local, mesh.shape["ctx"], mesh.shape["tp"], mesh.shape["dp"])
    return jax.shard_map(body, mesh=mesh, in_specs=in_specs, out_specs=out_specs, check_vma=False)
```

```python
import functools
import math

import jax
import jax.numpy as jnp
import numpy as np
from jax import lax
from jax.experimental import pallas as pl
from jax.experimental.pallas import tpu as pltpu
from jax.sharding import PartitionSpec as P

TAPS = 7


exact_mode = lax.Precision.HIGHEST


def passed_along(block, axis, distance):
    devices = range(lax.axis_size(axis))
    route = [(i - distance, i) for i in devices if i - distance in devices]
    return lax.ppermute(block, axis, route)


def phase_table(left_index, right_index, period, sign_factor):
    turns = left_index * right_index % period
    angle = 2.0 * math.pi / period * turns.astype(jnp.float32)
    return (jnp.cos(angle), sign_factor * jnp.sin(angle))


def complex_apply(form, table_real, table_imag, data_real, data_imag):
    out_real = jnp.einsum(form, table_real, data_real, precision=exact_mode) - jnp.einsum(
        form, table_imag, data_imag, precision=exact_mode
    )
    out_imag = jnp.einsum(form, table_real, data_imag, precision=exact_mode) + jnp.einsum(
        form, table_imag, data_real, precision=exact_mode
    )
    return (out_real, out_imag)


def small_factor(length_all):
    factor = 1
    for candidate in range(1, length_all + 1):
        if candidate * candidate > length_all:
            break
        if length_all % candidate == 0:
            factor = candidate
    return factor


def local_dft(real_part, imag_part, sign_factor):
    dims_in = real_part.shape
    length_all = dims_in[-2]
    factor_one = small_factor(length_all)
    factor_two = length_all // factor_one
    leading = dims_in[:-2]
    channels = dims_in[-1]
    real_view = real_part.reshape(leading + (factor_one, factor_two, channels))
    imag_view = imag_part.reshape(leading + (factor_one, factor_two, channels))
    index_one = jnp.arange(factor_one, dtype=jnp.int32)
    index_two = jnp.arange(factor_two, dtype=jnp.int32)
    cos_one, sin_one = phase_table(index_one[:, None], index_one[None, :], factor_one, sign_factor)
    section_real, section_imag = complex_apply(
        "kn,...nmc->...kmc", cos_one, sin_one, real_view, imag_view
    )
    twist_real, twist_imag = phase_table(
        index_one[:, None], index_two[None, :], length_all, sign_factor
    )
    twist_real = twist_real[..., None]
    twist_imag = twist_imag[..., None]
    turned_real = section_real * twist_real - section_imag * twist_imag
    turned_imag = section_real * twist_imag + section_imag * twist_real
    cos_two, sin_two = phase_table(index_two[:, None], index_two[None, :], factor_two, sign_factor)
    final_real, final_imag = complex_apply(
        "dm,...kmc->...dkc", cos_two, sin_two, turned_real, turned_imag
    )
    return (final_real.reshape(dims_in), final_imag.reshape(dims_in))


def split_channels_conv(gated, long_filter):
    signals = jnp.stack([gated, long_filter])
    columns = lax.all_to_all(signals, "ctx", split_axis=2, concat_axis=1, tiled=True)
    whole_rows = columns.shape[1]
    total_len = 2 * whole_rows
    padded = jnp.concatenate([columns, jnp.zeros_like(columns)], axis=1)
    spec_real, spec_imag = local_dft(padded, jnp.zeros_like(padded), -1.0)
    prod_real = spec_real[0] * spec_real[1] - spec_imag[0] * spec_imag[1]
    prod_imag = spec_real[0] * spec_imag[1] + spec_imag[0] * spec_real[1]
    back_real, back_imag = local_dft(prod_real, prod_imag, 1.0)
    result_cols = back_real[:whole_rows] * (1.0 / total_len)
    return lax.all_to_all(result_cols, "ctx", split_axis=0, concat_axis=1, tiled=True)


def plain_local(projected, short_taps, long_filter, skip_gain, w_out):
    seq_rows = projected.shape[1]
    prior = passed_along(projected[:, seq_rows - (TAPS - 1) :, :], "ctx", 1)
    extended = jnp.concatenate([prior, projected], axis=1).astype(jnp.float32)
    featured = short_taps[:, 0, None, :] * extended[:, TAPS - 1 : TAPS - 1 + seq_rows, :]
    for tap_index in range(1, TAPS):
        featured = (
            featured
            + short_taps[:, tap_index, None, :]
            * extended[:, TAPS - 1 - tap_index : TAPS - 1 - tap_index + seq_rows, :]
        )
    query = featured[0]
    gated = featured[1] * featured[2]
    long_conv = split_channels_conv(gated, long_filter)
    mixed = (query * (long_conv + skip_gain[None, :] * gated)).astype(jnp.bfloat16)
    partial_terms = jnp.dot(mixed, w_out, preferred_element_type=jnp.float32)
    return lax.psum_scatter(
        partial_terms.astype(jnp.bfloat16), "tp", scatter_dimension=1, tiled=True
    )


HALO = 8
STRIP = 32
PIECES = 4
UNITS = 8
HANDED = 2
SIDE = 2
LIMIT = 60 * 1024 * 1024
MESH_ID = pl.DeviceIdType.MESH


def block_tables(rows):
    length = 2 * rows
    k = np.arange(rows)[:, None]
    t = np.arange(rows)[None, :]
    angle = 2.0 * np.pi / length * (k * t % length)
    real, imag = np.cos(angle), -np.sin(angle)
    imag[0] = np.where(t[0] % 2 == 0, 1.0, -1.0)
    forward = np.concatenate([real, imag], axis=0)
    sign = np.where(k % 2 == 0, 1.0, -1.0)
    both = np.concatenate([forward * np.concatenate([sign, sign], axis=0), forward], axis=1)
    weight = np.where(k == 0, 1.0, 2.0) / length
    inverse = np.concatenate([real * weight, imag * weight], axis=0).T
    as_bf16 = lambda table: jnp.asarray(np.asarray(table, np.float32), jnp.bfloat16)
    return as_bf16(both), as_bf16(inverse)


def operator_kernel(
    n, m, p, proj_hbm, taps_hbm, filt_hbm, skip_hbm, w_hbm, both_hbm, inverse_hbm,
    own_hbm, got_hbm,
    proj, taps, filt, skip, both, inverse, w,
    halo, ext, gsend, hsend, hbuf, gall, gated, query, gspec, kspec, zspec,
    csend, conv, mixed, part, near_s, near_r, mix_r, far_s, far_r, home_s, handed,
    load_sem, out_sem, halo_sem, h_ss, h_rs, f_ss, f_rs, g_ss, g_rs, c_ss, c_rs,
    near_ss, near_rs, mix_ss, mix_rs, far_ss, far_rs, home_ss, home_rs,
    w_ss, w_rs, x_sem, s_ss, s_rs, b_ss, b_rs,
):
    me = lax.axis_index("ctx")
    z = lax.axis_index("tp")
    core = lax.axis_index("dp")
    rows, width = proj.shape[1], proj.shape[2]
    cols = width // n
    share = cols // p
    out_cols = own_hbm.shape[1]
    piece = rows // PIECES
    unit = rows // UNITS
    f32, bf16 = jnp.float32, jnp.bfloat16

    lower = 2 * z < m
    inner = jnp.where(lower, z, m - 1 - z)
    at_end = inner == 0
    at_mid = inner == 1
    pair = z + 1 - 2 * lax.rem(z, 2)
    across = m - 1 - z

    barrier = pltpu.get_barrier_semaphore()
    for k in range(1, n):
        pl.semaphore_signal(
            barrier, inc=1, device_id={"ctx": lax.rem(me + k, n)}, device_id_type=MESH_ID
        )
    for k in range(1, p):
        pl.semaphore_signal(
            barrier, inc=1, device_id={"dp": lax.rem(core + k, p)}, device_id_type=MESH_ID
        )
    pl.semaphore_signal(barrier, inc=1, device_id={"tp": pair}, device_id_type=MESH_ID)

    @pl.when(at_mid)
    def _():
        pl.semaphore_signal(barrier, inc=1, device_id={"tp": across}, device_id_type=MESH_ID)

    pairs = (
        (filt_hbm, filt), (proj_hbm, proj), (taps_hbm, taps), (both_hbm, both),
        (inverse_hbm, inverse), (skip_hbm, skip), (w_hbm, w),
    )
    loads = [pltpu.make_async_copy(a, b, load_sem.at[i]) for i, (a, b) in enumerate(pairs)]
    filt_load, proj_load, taps_load, both_load, inverse_load, skip_load, w_load = loads
    for load in (filt_load, proj_load, taps_load):
        load.start()

    filt_load.wait()
    for c in range(n):
        for q in range(p):
            at = c * cols + q * share
            hsend[c, q] = filt[:, at : at + share].astype(bf16)
    hbuf[0] = jnp.zeros((p, rows, share), bf16)
    hbuf[me + 1] = hsend[me]
    proj_load.wait()
    for load in (both_load, inverse_load, skip_load, w_load):
        load.start()

    pl.semaphore_wait(barrier, n - 1 + p - 1 + 1 + jnp.where(at_mid, 1, 0))

    halo_copy = pltpu.make_async_remote_copy(
        proj.at[:, rows - HALO :, :], halo, halo_sem.at[0], halo_sem.at[1],
        device_id={"ctx": lax.rem(me + 1, n)}, device_id_type=MESH_ID,
    )

    @pl.when(me < n - 1)
    def _():
        halo_copy.start()

    @pl.when(me == 0)
    def _():
        halo[...] = jnp.zeros_like(halo)

    group = width // (n * p)

    def whole(index, size):
        return pl.ds(pl.multiple_of(index * size, size), size)

    def real(d):
        return jnp.where(lower, d, m - 1 - d)

    def block(d):
        return whole(real(d), out_cols)

    def h_copy(k):
        c = lax.rem(me + k, n)
        return pltpu.make_async_remote_copy(
            hsend.at[c, core], hbuf.at[me + 1, core], h_ss.at[k], h_rs.at[k],
            device_id={"ctx": c}, device_id_type=MESH_ID,
        )

    def f_copy(k, q):
        b = lax.rem(me + n - k, n) + 1
        return pltpu.make_async_remote_copy(
            hbuf.at[b, core], hbuf.at[b, core], f_ss.at[k, q], f_rs.at[k, q],
            device_id={"dp": lax.rem(core + q, p)}, device_id_type=MESH_ID,
        )

    def g_copy(k):
        c = lax.rem(me + k, n)
        return pltpu.make_async_remote_copy(
            gsend.at[c], gall.at[me], g_ss.at[k], g_rs.at[k],
            device_id={"ctx": c}, device_id_type=MESH_ID,
        )

    def c_copy(r, k):
        c = lax.rem(me + k, n)
        span = whole(r, piece)
        return pltpu.make_async_remote_copy(
            csend.at[c, span], conv.at[me, span], c_ss.at[r, k], c_rs.at[r, k],
            device_id={"ctx": c}, device_id_type=MESH_ID,
        )

    def near_copy(u):
        return pltpu.make_async_remote_copy(
            near_s.at[whole(u, unit)], near_r.at[whole(u, unit)], near_ss.at[u], near_rs.at[u],
            device_id={"tp": pair}, device_id_type=MESH_ID,
        )

    def mix_copy(u):
        return pltpu.make_async_remote_copy(
            mixed.at[whole(u, unit)], mix_r.at[whole(u, unit)], mix_ss.at[u], mix_rs.at[u],
            device_id={"tp": pair}, device_id_type=MESH_ID,
        )

    def far_copy(v):
        return pltpu.make_async_remote_copy(
            far_s.at[whole(v, unit)], far_r.at[whole(v, unit)], far_ss.at[v], far_rs.at[v],
            device_id={"tp": across}, device_id_type=MESH_ID,
        )

    def got_copy(u):
        v = UNITS + u
        return pltpu.make_async_remote_copy(
            far_s.at[whole(v, unit)], got_hbm.at[whole(u, unit)], far_ss.at[v], far_rs.at[v],
            device_id={"tp": across}, device_id_type=MESH_ID,
        )

    def home_copy(u):
        return pltpu.make_async_remote_copy(
            home_s.at[whole(u, unit)], got_hbm.at[whole(u, unit)], home_ss.at[u], home_rs.at[u],
            device_id={"tp": pair}, device_id_type=MESH_ID,
        )

    beside = me + 1 - 2 * lax.rem(me, SIDE)
    above = lax.rem(me + SIDE, n)
    corner = lax.rem(beside + SIDE, n)
    plane = (me, beside, above, corner)
    half = group // 2
    quarter = group // 4

    def rows_of(k):
        return whole(plane[k] * p + core, group)

    def half_of(k, i):
        return whole((plane[k] * p + core) * 2 + i, half)

    def last_of(j, k, i):
        if j:
            return half_of(k, i)
        return whole((plane[k] * p + core) * 4 + 3 * i, quarter)

    def x_copy():
        start = ((corner * p + core) * 4 + 1) * quarter
        at = pl.ds(pl.multiple_of(start, quarter), half)
        return pltpu.make_async_remote_copy(
            w_hbm.at[at, block(m - 2)], handed.at[0, at], x_sem.at[0], x_sem.at[1],
            device_id={"tp": pair}, device_id_type=MESH_ID,
        )

    def w_copy(j):
        return pltpu.make_async_remote_copy(
            w_hbm.at[rows_of(0), block(m - 2 - j)], handed.at[j, rows_of(0)],
            w_ss.at[j], w_rs.at[j], device_id={"tp": pair}, device_id_type=MESH_ID,
        )

    def s_copy(j, k, i):
        if i < 2:
            at = half_of(0, i if k == 0 else 1 - i)
        else:
            at = last_of(j, 2, 1) if k == 0 else last_of(j, 1, 0)
        return pltpu.make_async_remote_copy(
            handed.at[j, at], handed.at[j, at], s_ss.at[j, k, i], s_rs.at[j, k, i],
            device_id={"ctx": (beside, above)[k]}, device_id_type=MESH_ID,
        )

    middle = pl.ds(
        pl.multiple_of(((corner * p + core) * 4 + 1) * quarter, quarter), half
    )

    def b_copy(j, i, q):
        at = (
            rows_of(0), half_of(1, 0), half_of(2, 1), half_of(1, 1), half_of(2, 0),
            last_of(j, 3, 1), last_of(j, 3, 0), middle,
        )[i]
        return pltpu.make_async_remote_copy(
            handed.at[j, at], handed.at[j, at], b_ss.at[j, i, q], b_rs.at[j, i, q],
            device_id={"dp": lax.rem(core + q, p)}, device_id_type=MESH_ID,
        )

    def share_out(j, i):
        for q in range(1, p):
            b_copy(j, i, q).start()

    def own_copy(d):
        return pltpu.make_async_copy(part.at[d], own_hbm, out_sem)

    for k in range(1, n):
        h_copy(k).start()

    @pl.when(at_end)
    def _():
        w_copy(0).start()
        x_copy().start()
        w_copy(1).start()

    def features(i, start, span):
        total = None
        for j in range(TAPS):
            term = taps[i, pl.ds(j, 1), span] * ext[i, pl.ds(HALO + start - j, STRIP), :]
            total = term if total is None else total + term
        return total

    def fill_body(i, span):
        ext[i, HALO:, :] = proj[i, :, span].astype(f32)

    def fill_head(i, span):
        ext[i, :HALO, :] = halo[i, :, span].astype(f32)

    taps_load.wait()

    def gate_block(k, _):
        c = lax.rem(me + 1 + k, n)
        span = whole(c, cols)
        fill_body(1, span)
        fill_body(2, span)

        def strip(start):
            value = features(1, start, span) * features(2, start, span)
            gated[start : start + STRIP, span] = value
            gsend[c, start : start + STRIP, :] = value.astype(bf16)

        for start in reversed(range(STRIP, rows, STRIP)):
            strip(start)

        @pl.when((k == 0) & (me > 0))
        def _():
            halo_copy.wait_recv()

        fill_head(1, span)
        fill_head(2, span)
        strip(0)

        @pl.when(k < n - 1)
        def _():
            g_copy(k + 1).start()

        return 0

    lax.fori_loop(0, n, gate_block, 0)
    gall[me] = gsend[me]

    def query_block(c, _):
        span = whole(c, cols)
        fill_body(0, span)
        fill_head(0, span)
        for start in range(0, rows, STRIP):
            query[start : start + STRIP, span] = features(0, start, span)
        return 0

    for k in range(1, n):
        h_copy(k).wait_recv()
        for q in range(1, p):
            f_copy(k, q).start()

    lax.fori_loop(0, n, query_block, 0)

    for k in range(1, n):
        for q in range(1, p):
            f_copy(k, q).wait_recv()
    both_load.wait()

    def begin(j):
        w_copy(j).wait_recv()
        for k in range(2):
            s_copy(j, k, 0).start()
        share_out(j, 0)

    first_row = lax.broadcasted_iota(jnp.int32, (rows, cols), 0) == 0

    def filter_spectrum(b, _):
        two = jnp.concatenate(
            [hbuf[pl.ds(b, 2), q].reshape(2 * rows, share) for q in range(p)], axis=1
        )
        spec = jnp.dot(both[...], two, preferred_element_type=f32)
        re, im = spec[:rows], spec[rows:]
        kspec[b, 0] = re
        kspec[b, 1] = jnp.where(first_row, 0.0, im)
        kspec[b, 2] = jnp.where(first_row, im, re)
        return 0

    @pl.when(at_mid)
    def _():
        begin(0)

    lax.fori_loop(0, n, filter_spectrum, 0, unroll=True)

    def signal_spectrum(k, _):
        b = lax.rem(me + n - k, n)

        @pl.when(k > 0)
        def _():
            g_copy(k).wait_recv()

        gspec[b] = jnp.dot(both[:, rows:], gall[b], preferred_element_type=f32)
        return 0

    lax.fori_loop(0, n, signal_spectrum, 0)

    def product(s, _):
        real_at = whole(s, 16)
        imag_at = pl.ds(pl.multiple_of(rows + s * 16, 16), 16)
        for lane in range(0, cols, 128):
            lanes = slice(lane, lane + 128)
            g_re = [gspec[b, real_at, lanes] for b in range(n)]
            g_im = [gspec[b, imag_at, lanes] for b in range(n)]
            k_re = [kspec[b, 0, real_at, lanes] for b in range(n)]
            k_im = [kspec[b, 1, real_at, lanes] for b in range(n)]
            k_alt = [kspec[b, 2, real_at, lanes] for b in range(n)]
            for i in range(n):
                z_re = z_im = None
                for j in range(i + 1):
                    t_re = g_re[j] * k_re[i - j] - g_im[j] * k_im[i - j]
                    t_im = g_re[j] * k_im[i - j] + g_im[j] * k_alt[i - j]
                    z_re = t_re if z_re is None else z_re + t_re
                    z_im = t_im if z_im is None else z_im + t_im
                zspec[i, real_at, lanes] = z_re.astype(bf16)
                zspec[i, imag_at, lanes] = z_im.astype(bf16)
        return 0

    lax.fori_loop(0, rows // 16, product, 0, unroll=4)
    inverse_load.wait()

    def back(r, _):
        span = whole(r, piece)
        for k in range(n):
            c = lax.rem(me + 1 + k, n)
            value = jnp.dot(inverse[span, :], zspec[c], preferred_element_type=f32).astype(bf16)
            if k < n - 1:
                csend[c, span, :] = value
                c_copy(r, k + 1).start()
            else:
                conv[me, span, :] = value
        return 0

    lax.fori_loop(0, PIECES, back, 0)

    def spread(j):
        if j:
            begin(j)
        for k in range(2):
            s_copy(j, k, 1).start()
        if j == 0:
            x_copy().wait_recv()
            share_out(0, 7)

    def relay(j):
        for k in range(2):
            s_copy(j, k, 0).wait_recv()
            s_copy(j, 1 - k, 2).start()
            share_out(j, 1 + k)

    def forward(j):
        for k in range(2):
            s_copy(j, k, 1).wait_recv()
            share_out(j, 3 + k)

    def corner_in(j):
        for k in range(2):
            s_copy(j, k, 2).wait_recv()
            share_out(j, 5 + k)

    def settle(j):
        for i in range(7 + (j == 0)):
            for q in range(1, p):
                b_copy(j, i, q).wait_recv()

    skip_load.wait()
    w_load.wait()

    @pl.when(at_mid)
    def _():
        spread(0)

    def mix_piece(r):
        span = whole(r, piece)
        for k in range(1, n):
            c_copy(r, k).wait_recv()
        for c in range(n):
            at = slice(c * cols, (c + 1) * cols)
            mixed[span, at] = (
                query[span, at]
                * (conv[c, span, :].astype(f32) + skip[:, at] * gated[span, at])
            ).astype(bf16)
        value = jnp.dot(mixed[span, :], w[:, block(m - 1)], preferred_element_type=f32)

        @pl.when(at_end)
        def _():
            near_s[span, :] = value.astype(bf16)
            for u in range(UNITS // PIECES):
                near_copy(r * (UNITS // PIECES) + u).start()

        @pl.when(at_mid)
        def _():
            part[m - 1, span, :] = value

    def own_part(d):
        part[d] = jnp.dot(mixed[...], w[:, block(d)], preferred_element_type=f32)

    def drain_front():
        @pl.when(me < n - 1)
        def _():
            halo_copy.wait_send()

        for k in range(1, n):
            h_copy(k).wait_send()
            for q in range(1, p):
                f_copy(k, q).wait_send()
            g_copy(k).wait_send()
            for r in range(PIECES):
                c_copy(r, k).wait_send()

    def ends():
        def first(r, _):
            mix_piece(r)
            return 0

        lax.fori_loop(0, PIECES, first, 0)

        def give(u, _):
            mix_copy(u).start()
            return 0

        lax.fori_loop(0, UNITS, give, 0)
        own_part(0)
        own_copy(0).start()

        drain_front()
        for j in range(HANDED):
            w_copy(j).wait_send()
        x_copy().wait_send()
        own_copy(0).wait()
        for u in range(UNITS):
            near_copy(u).wait_send()
            mix_copy(u).wait_send()

        def last(u, _):
            home_copy(u).wait_recv()
            return 0

        lax.fori_loop(0, UNITS, last, 0)

    def mids():
        def step(s, _):
            @pl.when(s == UNITS + 2)
            def _():
                settle(0)

            v = s - 2

            @pl.when((v >= 0) & (v < UNITS))
            def _():
                at = whole(v, unit)
                near_copy(v).wait_recv()
                far_s[at, :] = (part[m - 1, at, :] + near_r[at, :].astype(f32)).astype(bf16)
                far_copy(v).start()

            @pl.when((v >= UNITS) & (v < 2 * UNITS))
            def _():
                u = v - UNITS
                at = whole(u, unit)
                mix_copy(u).wait_recv()
                value = jnp.dot(mix_r[at, :], handed[0], preferred_element_type=f32)
                far_s[whole(v, unit), :] = (part[2, at, :] + value).astype(bf16)
                got_copy(u).start()

            @pl.when(s == UNITS - 6)
            def _():
                relay(0)
                spread(1)

            @pl.when(s == UNITS - 4)
            def _():
                forward(0)

            @pl.when(s == UNITS - 2)
            def _():
                corner_in(0)

            @pl.when(s == UNITS + 4)
            def _():
                relay(1)

            @pl.when(s == UNITS + 6)
            def _():
                forward(1)

            @pl.when(s == UNITS + 9)
            def _():
                corner_in(1)

            @pl.when(s < PIECES)
            def _():
                mix_piece(s)

            @pl.when(s == PIECES + 1)
            def _():
                own_part(2)

            @pl.when(s == PIECES + 2)
            def _():
                own_part(1)

            @pl.when(s == PIECES)
            def _():
                own_part(0)

            @pl.when((v >= 3) & (v < UNITS + 3))
            def _():
                u = v - 3
                at = whole(u, unit)
                far_copy(u).wait_recv()
                home_s[at, :] = (part[0, at, :] + far_r[at, :].astype(f32)).astype(bf16)
                home_copy(u).start()

            return 0

        lax.fori_loop(0, 2 * UNITS + 2, step, 0)
        settle(1)
        part[1] = part[1] + jnp.dot(mix_r[...], handed[1], preferred_element_type=f32)

        own_copy(1).start()

        drain_front()
        for j in range(HANDED):
            for k in range(2):
                for i in range(3):
                    s_copy(j, k, i).wait_send()
            for i in range(7 + (j == 0)):
                for q in range(1, p):
                    b_copy(j, i, q).wait_send()
        for u in range(UNITS):
            home_copy(u).wait_send()
            far_copy(u).wait_send()
        for u in range(UNITS - 1):
            got_copy(u).wait_send()
            got_copy(u).wait_recv()
        own_copy(1).wait()
        got_copy(UNITS - 1).wait_send()
        got_copy(UNITS - 1).wait_recv()

    pl.when(at_end)(ends)
    pl.when(at_mid)(mids)


def scratch_of(n, m, p, rows, width, all_out):
    cols, out_cols = width // n, all_out // m
    f32, bf16 = jnp.float32, jnp.bfloat16
    return [
        ((3, rows, width), bf16),
        ((3, TAPS, width), f32),
        ((rows, width), f32),
        ((1, width), f32),
        ((2 * rows, 2 * rows), bf16),
        ((rows, 2 * rows), bf16),
        ((width, all_out), bf16),
        ((3, HALO, width), bf16),
        ((3, HALO + rows, cols), f32),
        ((n, rows, cols), bf16),
        ((n, p, rows, cols // p), bf16),
        ((n + 1, p, rows, cols // p), bf16),
        ((n, rows, cols), bf16),
        ((rows, width), f32),
        ((rows, width), f32),
        ((n, 2 * rows, cols), f32),
        ((n, 3, rows, cols), f32),
        ((n, 2 * rows, cols), bf16),
        ((n, rows, cols), bf16),
        ((n, rows, cols), bf16),
        ((rows, width), bf16),
        ((m, rows, out_cols), f32),
        ((rows, out_cols), bf16),
        ((rows, out_cols), bf16),
        ((rows, width), bf16),
        ((2 * rows, out_cols), bf16),
        ((rows, out_cols), bf16),
        ((rows, out_cols), bf16),
        ((HANDED, width, out_cols), bf16),
    ]


def fused_local(n, m, p, projected, short_taps, long_filter, skip_gain, w_out):
    rows, width = projected.shape[1:]
    all_out = w_out.shape[1]
    both, inverse = block_tables(rows)
    anywhere = pl.BlockSpec(memory_space=pl.ANY)
    counts = [
        (7,), (), (2,), (n,), (n,), (n, p), (n, p), (n,), (n,), (PIECES, n), (PIECES, n),
        (UNITS,), (UNITS,), (UNITS,), (UNITS,), (2 * UNITS,), (2 * UNITS,), (UNITS,), (UNITS,),
        (HANDED,), (HANDED,), (2,), (HANDED, 2, 3), (HANDED, 2, 3), (HANDED, 8, p), (HANDED, 8, p),
    ]
    shape = (rows, all_out // m)
    own, got = pl.pallas_call(
        functools.partial(operator_kernel, n, m, p),
        out_shape=(
            jax.ShapeDtypeStruct(shape, jnp.float32),
            jax.ShapeDtypeStruct(shape, jnp.bfloat16),
        ),
        in_specs=[anywhere] * 7,
        out_specs=(anywhere, anywhere),
        scratch_shapes=[pltpu.VMEM(*one) for one in scratch_of(n, m, p, rows, width, all_out)]
        + [pltpu.SemaphoreType.DMA(count) for count in counts],
        compiler_params=pltpu.CompilerParams(
            collective_id=0, has_side_effects=True, vmem_limit_bytes=LIMIT
        ),
    )(projected, short_taps, long_filter, skip_gain.reshape(1, width), w_out, both, inverse)
    return (own + got.astype(jnp.float32)).astype(jnp.bfloat16)


def fits_kernel(n, m, p, rows, width, all_out):
    if n != SIDE * SIDE or m != HANDED + 2 or width % (128 * n * p) or all_out % (128 * m):
        return False
    if rows % (16 * UNITS) or rows % STRIP or rows % (16 * PIECES):
        return False
    held = sum(
        math.prod(shape) * jnp.dtype(kind).itemsize
        for shape, kind in scratch_of(n, m, p, rows, width, all_out)
    )
    return held + 12 * 1024 * 1024 < LIMIT


def local(n, m, p, projected, short_taps, long_filter, skip_gain, w_out):
    rows, width = projected.shape[1:]
    if fits_kernel(n, m, p, rows, width, w_out.shape[1]):
        return fused_local(n, m, p, projected, short_taps, long_filter, skip_gain, w_out)
    return plain_local(projected, short_taps, long_filter, skip_gain, w_out)


def solution(mesh):
    in_specs = (
        P(None, ("dp", "ctx"), "tp"),
        P(None, None, "tp"),
        P("ctx", "tp"),
        P("tp"),
        P("tp", None),
    )
    out_specs = P(("dp", "ctx"), "tp")
    body = functools.partial(local, mesh.shape["ctx"], mesh.shape["tp"], mesh.shape["dp"])
    return jax.shard_map(body, mesh=mesh, in_specs=in_specs, out_specs=out_specs, check_vma=False)
```

```python
import functools
import math

import jax
import jax.numpy as jnp
import numpy as np
from jax import lax
from jax.experimental import pallas as pl
from jax.experimental.pallas import tpu as pltpu
from jax.sharding import PartitionSpec as P

TAPS = 7


exact_mode = lax.Precision.HIGHEST


def passed_along(block, axis, distance):
    devices = range(lax.axis_size(axis))
    route = [(i - distance, i) for i in devices if i - distance in devices]
    return lax.ppermute(block, axis, route)


def phase_table(left_index, right_index, period, sign_factor):
    turns = left_index * right_index % period
    angle = 2.0 * math.pi / period * turns.astype(jnp.float32)
    return (jnp.cos(angle), sign_factor * jnp.sin(angle))


def complex_apply(form, table_real, table_imag, data_real, data_imag):
    out_real = jnp.einsum(form, table_real, data_real, precision=exact_mode) - jnp.einsum(
        form, table_imag, data_imag, precision=exact_mode
    )
    out_imag = jnp.einsum(form, table_real, data_imag, precision=exact_mode) + jnp.einsum(
        form, table_imag, data_real, precision=exact_mode
    )
    return (out_real, out_imag)


def small_factor(length_all):
    factor = 1
    for candidate in range(1, length_all + 1):
        if candidate * candidate > length_all:
            break
        if length_all % candidate == 0:
            factor = candidate
    return factor


def local_dft(real_part, imag_part, sign_factor):
    dims_in = real_part.shape
    length_all = dims_in[-2]
    factor_one = small_factor(length_all)
    factor_two = length_all // factor_one
    leading = dims_in[:-2]
    channels = dims_in[-1]
    real_view = real_part.reshape(leading + (factor_one, factor_two, channels))
    imag_view = imag_part.reshape(leading + (factor_one, factor_two, channels))
    index_one = jnp.arange(factor_one, dtype=jnp.int32)
    index_two = jnp.arange(factor_two, dtype=jnp.int32)
    cos_one, sin_one = phase_table(index_one[:, None], index_one[None, :], factor_one, sign_factor)
    section_real, section_imag = complex_apply(
        "kn,...nmc->...kmc", cos_one, sin_one, real_view, imag_view
    )
    twist_real, twist_imag = phase_table(
        index_one[:, None], index_two[None, :], length_all, sign_factor
    )
    twist_real = twist_real[..., None]
    twist_imag = twist_imag[..., None]
    turned_real = section_real * twist_real - section_imag * twist_imag
    turned_imag = section_real * twist_imag + section_imag * twist_real
    cos_two, sin_two = phase_table(index_two[:, None], index_two[None, :], factor_two, sign_factor)
    final_real, final_imag = complex_apply(
        "dm,...kmc->...dkc", cos_two, sin_two, turned_real, turned_imag
    )
    return (final_real.reshape(dims_in), final_imag.reshape(dims_in))


def split_channels_conv(gated, long_filter):
    signals = jnp.stack([gated, long_filter])
    columns = lax.all_to_all(signals, "ctx", split_axis=2, concat_axis=1, tiled=True)
    whole_rows = columns.shape[1]
    total_len = 2 * whole_rows
    padded = jnp.concatenate([columns, jnp.zeros_like(columns)], axis=1)
    spec_real, spec_imag = local_dft(padded, jnp.zeros_like(padded), -1.0)
    prod_real = spec_real[0] * spec_real[1] - spec_imag[0] * spec_imag[1]
    prod_imag = spec_real[0] * spec_imag[1] + spec_imag[0] * spec_real[1]
    back_real, back_imag = local_dft(prod_real, prod_imag, 1.0)
    result_cols = back_real[:whole_rows] * (1.0 / total_len)
    return lax.all_to_all(result_cols, "ctx", split_axis=0, concat_axis=1, tiled=True)


def plain_local(projected, short_taps, long_filter, skip_gain, w_out):
    seq_rows = projected.shape[1]
    prior = passed_along(projected[:, seq_rows - (TAPS - 1) :, :], "ctx", 1)
    extended = jnp.concatenate([prior, projected], axis=1).astype(jnp.float32)
    featured = short_taps[:, 0, None, :] * extended[:, TAPS - 1 : TAPS - 1 + seq_rows, :]
    for tap_index in range(1, TAPS):
        featured = (
            featured
            + short_taps[:, tap_index, None, :]
            * extended[:, TAPS - 1 - tap_index : TAPS - 1 - tap_index + seq_rows, :]
        )
    query = featured[0]
    gated = featured[1] * featured[2]
    long_conv = split_channels_conv(gated, long_filter)
    mixed = (query * (long_conv + skip_gain[None, :] * gated)).astype(jnp.bfloat16)
    partial_terms = jnp.dot(mixed, w_out, preferred_element_type=jnp.float32)
    return lax.psum_scatter(
        partial_terms.astype(jnp.bfloat16), "tp", scatter_dimension=1, tiled=True
    )


HALO = 8
STRIP = 32
PIECES = 4
UNITS = 8
HANDED = 2
SIDE = 2
LIMIT = 60 * 1024 * 1024
MESH_ID = pl.DeviceIdType.MESH


def block_tables(rows):
    length = 2 * rows
    k = np.arange(rows)[:, None]
    t = np.arange(rows)[None, :]
    angle = 2.0 * np.pi / length * (k * t % length)
    real, imag = np.cos(angle), -np.sin(angle)
    imag[0] = np.where(t[0] % 2 == 0, 1.0, -1.0)
    forward = np.concatenate([real, imag], axis=0)
    sign = np.where(k % 2 == 0, 1.0, -1.0)
    both = np.concatenate([forward * np.concatenate([sign, sign], axis=0), forward], axis=1)
    weight = np.where(k == 0, 1.0, 2.0) / length
    inverse = np.concatenate([real * weight, imag * weight], axis=0).T
    as_bf16 = lambda table: jnp.asarray(np.asarray(table, np.float32), jnp.bfloat16)
    return as_bf16(both), as_bf16(inverse)


def operator_kernel(
    n, m, p, proj_hbm, taps_hbm, filt_hbm, skip_hbm, w_hbm, both_hbm, inverse_hbm,
    own_hbm, got_hbm,
    proj, taps, filt, skip, both, inverse, w,
    halo, ext, gsend, hsend, hbuf, gall, gated, query, gspec, kspec, zspec,
    csend, conv, mixed, part, near_s, near_r, mix_r, far_s, far_r, home_s, handed,
    load_sem, out_sem, halo_sem, h_ss, h_rs, f_ss, f_rs, g_ss, g_rs, c_ss, c_rs, lead_ss, lead_rs,
    near_ss, near_rs, mix_ss, mix_rs, far_ss, far_rs, home_ss, home_rs,
    w_ss, w_rs, x_sem, s_ss, s_rs, b_ss, b_rs,
):
    me = lax.axis_index("ctx")
    z = lax.axis_index("tp")
    core = lax.axis_index("dp")
    rows, width = proj.shape[1], proj.shape[2]
    cols = width // n
    share = cols // p
    out_cols = own_hbm.shape[1]
    piece = rows // PIECES
    per = UNITS // PIECES
    unit = rows // UNITS
    f32, bf16 = jnp.float32, jnp.bfloat16

    lower = 2 * z < m
    inner = jnp.where(lower, z, m - 1 - z)
    at_end = inner == 0
    at_mid = inner == 1
    pair = z + 1 - 2 * lax.rem(z, 2)
    across = m - 1 - z

    barrier = pltpu.get_barrier_semaphore()
    for k in range(1, n):
        pl.semaphore_signal(
            barrier, inc=1, device_id={"ctx": lax.rem(me + k, n)}, device_id_type=MESH_ID
        )
    for k in range(1, p):
        pl.semaphore_signal(
            barrier, inc=1, device_id={"dp": lax.rem(core + k, p)}, device_id_type=MESH_ID
        )
    pl.semaphore_signal(barrier, inc=1, device_id={"tp": pair}, device_id_type=MESH_ID)

    @pl.when(at_mid)
    def _():
        pl.semaphore_signal(barrier, inc=1, device_id={"tp": across}, device_id_type=MESH_ID)

    pairs = (
        (filt_hbm, filt), (proj_hbm, proj), (taps_hbm, taps), (both_hbm, both),
        (inverse_hbm, inverse), (skip_hbm, skip), (w_hbm, w),
    )
    loads = [pltpu.make_async_copy(a, b, load_sem.at[i]) for i, (a, b) in enumerate(pairs)]
    filt_load, proj_load, taps_load, both_load, inverse_load, skip_load, w_load = loads
    for load in (filt_load, proj_load, taps_load):
        load.start()

    filt_load.wait()
    for c in range(n):
        for q in range(p):
            at = c * cols + q * share
            hsend[c, q] = filt[:, at : at + share].astype(bf16)
    hbuf[0] = jnp.zeros((p, rows, share), bf16)
    hbuf[me + 1] = hsend[me]
    proj_load.wait()
    for load in (both_load, inverse_load, skip_load, w_load):
        load.start()

    pl.semaphore_wait(barrier, n - 1 + p - 1 + 1 + jnp.where(at_mid, 1, 0))

    halo_copy = pltpu.make_async_remote_copy(
        proj.at[:, rows - HALO :, :], halo, halo_sem.at[0], halo_sem.at[1],
        device_id={"ctx": lax.rem(me + 1, n)}, device_id_type=MESH_ID,
    )

    @pl.when(me < n - 1)
    def _():
        halo_copy.start()

    @pl.when(me == 0)
    def _():
        halo[...] = jnp.zeros_like(halo)

    group = width // (n * p)

    def whole(index, size):
        return pl.ds(pl.multiple_of(index * size, size), size)

    def real(d):
        return jnp.where(lower, d, m - 1 - d)

    def block(d):
        return whole(real(d), out_cols)

    def h_copy(k):
        c = lax.rem(me + k, n)
        return pltpu.make_async_remote_copy(
            hsend.at[c, core], hbuf.at[me + 1, core], h_ss.at[k], h_rs.at[k],
            device_id={"ctx": c}, device_id_type=MESH_ID,
        )

    def f_copy(k, q):
        b = lax.rem(me + n - k, n) + 1
        return pltpu.make_async_remote_copy(
            hbuf.at[b, core], hbuf.at[b, core], f_ss.at[k, q], f_rs.at[k, q],
            device_id={"dp": lax.rem(core + q, p)}, device_id_type=MESH_ID,
        )

    def g_copy(k):
        c = lax.rem(me + k, n)
        return pltpu.make_async_remote_copy(
            gsend.at[c], gall.at[me], g_ss.at[k], g_rs.at[k],
            device_id={"ctx": c}, device_id_type=MESH_ID,
        )

    def c_copy(r, k):
        c = lax.rem(me + k, n)
        span = whole(r, piece)
        return pltpu.make_async_remote_copy(
            csend.at[c, span], conv.at[me, span], c_ss.at[r, k], c_rs.at[r, k],
            device_id={"ctx": c}, device_id_type=MESH_ID,
        )

    def lead_copy(i, k):
        c = lax.rem(me + k, n)
        span = whole(i, unit)
        return pltpu.make_async_remote_copy(
            csend.at[c, span], conv.at[me, span], lead_ss.at[i, k], lead_rs.at[i, k],
            device_id={"ctx": c}, device_id_type=MESH_ID,
        )

    def near_copy(u):
        return pltpu.make_async_remote_copy(
            near_s.at[whole(u, unit)], near_r.at[whole(u, unit)], near_ss.at[u], near_rs.at[u],
            device_id={"tp": pair}, device_id_type=MESH_ID,
        )

    def mix_copy(u):
        return pltpu.make_async_remote_copy(
            mixed.at[whole(u, unit)], mix_r.at[whole(u, unit)], mix_ss.at[u], mix_rs.at[u],
            device_id={"tp": pair}, device_id_type=MESH_ID,
        )

    def far_copy(v):
        return pltpu.make_async_remote_copy(
            far_s.at[whole(v, unit)], far_r.at[whole(v, unit)], far_ss.at[v], far_rs.at[v],
            device_id={"tp": across}, device_id_type=MESH_ID,
        )

    def got_copy(u):
        v = UNITS + u
        return pltpu.make_async_remote_copy(
            far_s.at[whole(v, unit)], got_hbm.at[whole(u, unit)], far_ss.at[v], far_rs.at[v],
            device_id={"tp": across}, device_id_type=MESH_ID,
        )

    def home_copy(u):
        return pltpu.make_async_remote_copy(
            home_s.at[whole(u, unit)], got_hbm.at[whole(u, unit)], home_ss.at[u], home_rs.at[u],
            device_id={"tp": pair}, device_id_type=MESH_ID,
        )

    beside = me + 1 - 2 * lax.rem(me, SIDE)
    above = lax.rem(me + SIDE, n)
    corner = lax.rem(beside + SIDE, n)
    plane = (me, beside, above, corner)
    half = group // 2
    quarter = group // 4

    def rows_of(k):
        return whole(plane[k] * p + core, group)

    def half_of(k, i):
        return whole((plane[k] * p + core) * 2 + i, half)

    def last_of(j, k, i):
        if j:
            return half_of(k, i)
        return whole((plane[k] * p + core) * 4 + 3 * i, quarter)

    def x_copy():
        start = ((corner * p + core) * 4 + 1) * quarter
        at = pl.ds(pl.multiple_of(start, quarter), half)
        return pltpu.make_async_remote_copy(
            w_hbm.at[at, block(m - 2)], handed.at[0, at], x_sem.at[0], x_sem.at[1],
            device_id={"tp": pair}, device_id_type=MESH_ID,
        )

    def w_copy(j):
        return pltpu.make_async_remote_copy(
            w_hbm.at[rows_of(0), block(m - 2 - j)], handed.at[j, rows_of(0)],
            w_ss.at[j], w_rs.at[j], device_id={"tp": pair}, device_id_type=MESH_ID,
        )

    def s_copy(j, k, i):
        if i < 2:
            at = half_of(0, i if k == 0 else 1 - i)
        else:
            at = last_of(j, 2, 1) if k == 0 else last_of(j, 1, 0)
        return pltpu.make_async_remote_copy(
            handed.at[j, at], handed.at[j, at], s_ss.at[j, k, i], s_rs.at[j, k, i],
            device_id={"ctx": (beside, above)[k]}, device_id_type=MESH_ID,
        )

    middle = pl.ds(
        pl.multiple_of(((corner * p + core) * 4 + 1) * quarter, quarter), half
    )

    def b_copy(j, i, q):
        at = (
            rows_of(0), half_of(1, 0), half_of(2, 1), half_of(1, 1), half_of(2, 0),
            last_of(j, 3, 1), last_of(j, 3, 0), middle,
        )[i]
        return pltpu.make_async_remote_copy(
            handed.at[j, at], handed.at[j, at], b_ss.at[j, i, q], b_rs.at[j, i, q],
            device_id={"dp": lax.rem(core + q, p)}, device_id_type=MESH_ID,
        )

    def share_out(j, i):
        for q in range(1, p):
            b_copy(j, i, q).start()

    def own_copy(d):
        return pltpu.make_async_copy(part.at[d], own_hbm, out_sem)

    for k in range(1, n):
        h_copy(k).start()

    @pl.when(at_end)
    def _():
        w_copy(0).start()
        x_copy().start()
        w_copy(1).start()

    def features(i, start, span):
        total = None
        for j in range(TAPS):
            term = taps[i, pl.ds(j, 1), span] * ext[i, pl.ds(HALO + start - j, STRIP), :]
            total = term if total is None else total + term
        return total

    def fill_body(i, span):
        ext[i, HALO:, :] = proj[i, :, span].astype(f32)

    def fill_head(i, span):
        ext[i, :HALO, :] = halo[i, :, span].astype(f32)

    taps_load.wait()

    def gate_block(k, _):
        c = lax.rem(me + 1 + k, n)
        span = whole(c, cols)
        fill_body(1, span)
        fill_body(2, span)

        def strip(start):
            value = features(1, start, span) * features(2, start, span)
            gated[start : start + STRIP, span] = value
            gsend[c, start : start + STRIP, :] = value.astype(bf16)

        for start in reversed(range(STRIP, rows, STRIP)):
            strip(start)

        @pl.when((k == 0) & (me > 0))
        def _():
            halo_copy.wait_recv()

        fill_head(1, span)
        fill_head(2, span)
        strip(0)

        @pl.when(k < n - 1)
        def _():
            g_copy(k + 1).start()

        return 0

    lax.fori_loop(0, n, gate_block, 0)
    gall[me] = gsend[me]

    def query_block(c, _):
        span = whole(c, cols)
        fill_body(0, span)
        fill_head(0, span)
        for start in range(0, rows, STRIP):
            query[start : start + STRIP, span] = features(0, start, span)
        return 0

    for k in range(1, n):
        h_copy(k).wait_recv()
        for q in range(1, p):
            f_copy(k, q).start()

    lax.fori_loop(0, n, query_block, 0)

    for k in range(1, n):
        for q in range(1, p):
            f_copy(k, q).wait_recv()
    both_load.wait()

    def begin(j):
        w_copy(j).wait_recv()
        for k in range(2):
            s_copy(j, k, 0).start()
        share_out(j, 0)

    first_row = lax.broadcasted_iota(jnp.int32, (rows, cols), 0) == 0

    def filter_spectrum(b, _):
        two = jnp.concatenate(
            [hbuf[pl.ds(b, 2), q].reshape(2 * rows, share) for q in range(p)], axis=1
        )
        spec = jnp.dot(both[...], two, preferred_element_type=f32)
        re, im = spec[:rows], spec[rows:]
        kspec[b, 0] = re
        kspec[b, 1] = jnp.where(first_row, 0.0, im)
        kspec[b, 2] = jnp.where(first_row, im, re)
        return 0

    @pl.when(at_mid)
    def _():
        begin(0)

    lax.fori_loop(0, n, filter_spectrum, 0, unroll=True)

    def signal_spectrum(k, _):
        b = lax.rem(me + n - k, n)

        @pl.when(k > 0)
        def _():
            g_copy(k).wait_recv()

        gspec[b] = jnp.dot(both[:, rows:], gall[b], preferred_element_type=f32)
        return 0

    lax.fori_loop(0, n, signal_spectrum, 0)

    def product(s, _):
        real_at = whole(s, 16)
        imag_at = pl.ds(pl.multiple_of(rows + s * 16, 16), 16)
        for lane in range(0, cols, 128):
            lanes = slice(lane, lane + 128)
            g_re = [gspec[b, real_at, lanes] for b in range(n)]
            g_im = [gspec[b, imag_at, lanes] for b in range(n)]
            k_re = [kspec[b, 0, real_at, lanes] for b in range(n)]
            k_im = [kspec[b, 1, real_at, lanes] for b in range(n)]
            k_alt = [kspec[b, 2, real_at, lanes] for b in range(n)]
            for i in range(n):
                z_re = z_im = None
                for j in range(i + 1):
                    t_re = g_re[j] * k_re[i - j] - g_im[j] * k_im[i - j]
                    t_im = g_re[j] * k_im[i - j] + g_im[j] * k_alt[i - j]
                    z_re = t_re if z_re is None else z_re + t_re
                    z_im = t_im if z_im is None else z_im + t_im
                zspec[i, real_at, lanes] = z_re.astype(bf16)
                zspec[i, imag_at, lanes] = z_im.astype(bf16)
        return 0

    lax.fori_loop(0, rows // 16, product, 0, unroll=4)
    inverse_load.wait()

    def back(r, _):
        span = whole(r, piece)
        for k in range(n):
            c = lax.rem(me + 1 + k, n)
            value = jnp.dot(inverse[span, :], zspec[c], preferred_element_type=f32).astype(bf16)
            if k < n - 1:
                csend[c, span, :] = value
                if not isinstance(r, int):
                    c_copy(r, k + 1).start()
            else:
                conv[me, span, :] = value
        return 0

    back(0, 0)
    for i in range(per):
        for k in range(1, n):
            lead_copy(i, k).start()
    lax.fori_loop(1, PIECES, back, 0)

    def spread(j):
        if j:
            begin(j)
        for k in range(2):
            s_copy(j, k, 1).start()
        if j == 0:
            x_copy().wait_recv()
            share_out(0, 7)

    def relay(j):
        for k in range(2):
            s_copy(j, k, 0).wait_recv()
            s_copy(j, 1 - k, 2).start()
            share_out(j, 1 + k)

    def forward(j):
        for k in range(2):
            s_copy(j, k, 1).wait_recv()
            share_out(j, 3 + k)

    def corner_in(j):
        for k in range(2):
            s_copy(j, k, 2).wait_recv()
            share_out(j, 5 + k)

    def settle(j):
        for i in range(7 + (j == 0)):
            for q in range(1, p):
                b_copy(j, i, q).wait_recv()

    skip_load.wait()
    w_load.wait()

    @pl.when(at_mid)
    def _():
        spread(0)

    def mix_rows(span):
        for c in range(n):
            at = slice(c * cols, (c + 1) * cols)
            mixed[span, at] = (
                query[span, at]
                * (conv[c, span, :].astype(f32) + skip[:, at] * gated[span, at])
            ).astype(bf16)
        return jnp.dot(mixed[span, :], w[:, block(m - 1)], preferred_element_type=f32)

    def mix_piece(r):
        span = whole(r, piece)
        for k in range(1, n):
            c_copy(r, k).wait_recv()
        value = mix_rows(span)

        @pl.when(at_end)
        def _():
            near_s[span, :] = value.astype(bf16)
            for u in range(per):
                near_copy(r * per + u).start()

        @pl.when(at_mid)
        def _():
            part[m - 1, span, :] = value

    def own_part(d):
        part[d] = jnp.dot(mixed[...], w[:, block(d)], preferred_element_type=f32)

    def drain_front():
        @pl.when(me < n - 1)
        def _():
            halo_copy.wait_send()

        for k in range(1, n):
            h_copy(k).wait_send()
            for q in range(1, p):
                f_copy(k, q).wait_send()
            g_copy(k).wait_send()
            for i in range(per):
                lead_copy(i, k).wait_send()
            for r in range(1, PIECES):
                c_copy(r, k).wait_send()

    def ends():
        def first(r, _):
            mix_piece(r)
            return 0

        for i in range(per):
            for k in range(1, n):
                lead_copy(i, k).wait_recv()
            near_s[whole(i, unit), :] = mix_rows(whole(i, unit)).astype(bf16)
            near_copy(i).start()
        lax.fori_loop(1, PIECES, first, 0)

        def give(u, _):
            mix_copy(u).start()
            return 0

        lax.fori_loop(0, UNITS, give, 0)
        own_part(0)
        own_copy(0).start()

        drain_front()
        for j in range(HANDED):
            w_copy(j).wait_send()
        x_copy().wait_send()
        own_copy(0).wait()
        for u in range(UNITS):
            near_copy(u).wait_send()
            mix_copy(u).wait_send()

        def last(u, _):
            home_copy(u).wait_recv()
            return 0

        lax.fori_loop(0, UNITS, last, 0)

    def mids():
        def step(s, _):
            @pl.when(s == UNITS + 2)
            def _():
                settle(0)

            v = s - 2

            @pl.when((v >= 0) & (v < UNITS))
            def _():
                at = whole(v, unit)
                near_copy(v).wait_recv()
                far_s[at, :] = (part[m - 1, at, :] + near_r[at, :].astype(f32)).astype(bf16)
                far_copy(v).start()

            @pl.when((v >= UNITS) & (v < 2 * UNITS))
            def _():
                u = v - UNITS
                at = whole(u, unit)
                mix_copy(u).wait_recv()
                value = jnp.dot(mix_r[at, :], handed[0], preferred_element_type=f32)
                far_s[whole(v, unit), :] = (part[2, at, :] + value).astype(bf16)
                got_copy(u).start()

            @pl.when(s == UNITS - 6)
            def _():
                relay(0)
                spread(1)

            @pl.when(s == UNITS - 4)
            def _():
                forward(0)

            @pl.when(s == UNITS - 2)
            def _():
                corner_in(0)

            @pl.when(s == UNITS + 4)
            def _():
                relay(1)

            @pl.when(s == UNITS + 6)
            def _():
                forward(1)

            @pl.when(s == UNITS + 9)
            def _():
                corner_in(1)

            @pl.when(s == 0)
            def _():
                for i in range(per):
                    for k in range(1, n):
                        lead_copy(i, k).wait_recv()
                part[m - 1, whole(0, piece), :] = mix_rows(whole(0, piece))

            @pl.when((s > 0) & (s < PIECES))
            def _():
                mix_piece(s)

            @pl.when(s == PIECES + 1)
            def _():
                own_part(2)

            @pl.when(s == PIECES + 2)
            def _():
                own_part(1)

            @pl.when(s == PIECES)
            def _():
                own_part(0)

            @pl.when((v >= 3) & (v < UNITS + 3))
            def _():
                u = v - 3
                at = whole(u, unit)
                far_copy(u).wait_recv()
                home_s[at, :] = (part[0, at, :] + far_r[at, :].astype(f32)).astype(bf16)
                home_copy(u).start()

            return 0

        lax.fori_loop(0, 2 * UNITS + 2, step, 0)
        settle(1)
        part[1] = part[1] + jnp.dot(mix_r[...], handed[1], preferred_element_type=f32)

        own_copy(1).start()

        drain_front()
        for j in range(HANDED):
            for k in range(2):
                for i in range(3):
                    s_copy(j, k, i).wait_send()
            for i in range(7 + (j == 0)):
                for q in range(1, p):
                    b_copy(j, i, q).wait_send()
        for u in range(UNITS):
            home_copy(u).wait_send()
            far_copy(u).wait_send()
        for u in range(UNITS - 1):
            got_copy(u).wait_send()
            got_copy(u).wait_recv()
        own_copy(1).wait()
        got_copy(UNITS - 1).wait_send()
        got_copy(UNITS - 1).wait_recv()

    pl.when(at_end)(ends)
    pl.when(at_mid)(mids)


def scratch_of(n, m, p, rows, width, all_out):
    cols, out_cols = width // n, all_out // m
    f32, bf16 = jnp.float32, jnp.bfloat16
    return [
        ((3, rows, width), bf16),
        ((3, TAPS, width), f32),
        ((rows, width), f32),
        ((1, width), f32),
        ((2 * rows, 2 * rows), bf16),
        ((rows, 2 * rows), bf16),
        ((width, all_out), bf16),
        ((3, HALO, width), bf16),
        ((3, HALO + rows, cols), f32),
        ((n, rows, cols), bf16),
        ((n, p, rows, cols // p), bf16),
        ((n + 1, p, rows, cols // p), bf16),
        ((n, rows, cols), bf16),
        ((rows, width), f32),
        ((rows, width), f32),
        ((n, 2 * rows, cols), f32),
        ((n, 3, rows, cols), f32),
        ((n, 2 * rows, cols), bf16),
        ((n, rows, cols), bf16),
        ((n, rows, cols), bf16),
        ((rows, width), bf16),
        ((m, rows, out_cols), f32),
        ((rows, out_cols), bf16),
        ((rows, out_cols), bf16),
        ((rows, width), bf16),
        ((2 * rows, out_cols), bf16),
        ((rows, out_cols), bf16),
        ((rows, out_cols), bf16),
        ((HANDED, width, out_cols), bf16),
    ]


def fused_local(n, m, p, projected, short_taps, long_filter, skip_gain, w_out):
    rows, width = projected.shape[1:]
    all_out = w_out.shape[1]
    both, inverse = block_tables(rows)
    anywhere = pl.BlockSpec(memory_space=pl.ANY)
    counts = [
        (7,), (), (2,), (n,), (n,), (n, p), (n, p), (n,), (n,), (PIECES, n), (PIECES, n),
        (UNITS // PIECES, n), (UNITS // PIECES, n),
        (UNITS,), (UNITS,), (UNITS,), (UNITS,), (2 * UNITS,), (2 * UNITS,), (UNITS,), (UNITS,),
        (HANDED,), (HANDED,), (2,), (HANDED, 2, 3), (HANDED, 2, 3), (HANDED, 8, p), (HANDED, 8, p),
    ]
    shape = (rows, all_out // m)
    own, got = pl.pallas_call(
        functools.partial(operator_kernel, n, m, p),
        out_shape=(
            jax.ShapeDtypeStruct(shape, jnp.float32),
            jax.ShapeDtypeStruct(shape, jnp.bfloat16),
        ),
        in_specs=[anywhere] * 7,
        out_specs=(anywhere, anywhere),
        scratch_shapes=[pltpu.VMEM(*one) for one in scratch_of(n, m, p, rows, width, all_out)]
        + [pltpu.SemaphoreType.DMA(count) for count in counts],
        compiler_params=pltpu.CompilerParams(
            collective_id=0, has_side_effects=True, vmem_limit_bytes=LIMIT
        ),
    )(projected, short_taps, long_filter, skip_gain.reshape(1, width), w_out, both, inverse)
    return (own + got.astype(jnp.float32)).astype(jnp.bfloat16)


def fits_kernel(n, m, p, rows, width, all_out):
    if n != SIDE * SIDE or m != HANDED + 2 or width % (128 * n * p) or all_out % (128 * m):
        return False
    if rows % (16 * UNITS) or rows % STRIP or rows % (16 * PIECES):
        return False
    held = sum(
        math.prod(shape) * jnp.dtype(kind).itemsize
        for shape, kind in scratch_of(n, m, p, rows, width, all_out)
    )
    return held + 12 * 1024 * 1024 < LIMIT


def local(n, m, p, projected, short_taps, long_filter, skip_gain, w_out):
    rows, width = projected.shape[1:]
    if fits_kernel(n, m, p, rows, width, w_out.shape[1]):
        return fused_local(n, m, p, projected, short_taps, long_filter, skip_gain, w_out)
    return plain_local(projected, short_taps, long_filter, skip_gain, w_out)


def solution(mesh):
    in_specs = (
        P(None, ("dp", "ctx"), "tp"),
        P(None, None, "tp"),
        P("ctx", "tp"),
        P("tp"),
        P("tp", None),
    )
    out_specs = P(("dp", "ctx"), "tp")
    body = functools.partial(local, mesh.shape["ctx"], mesh.shape["tp"], mesh.shape["dp"])
    return jax.shard_map(body, mesh=mesh, in_specs=in_specs, out_specs=out_specs, check_vma=False)
```
